32 devices in a mesh: expert: 16 (over z, y, x), replica: 2 (over core).
Axes of the slice: x: 2, y: 2, z: 4, core: 2. Of those that a mesh axis runs over, the one named last changes fastest.
Arguments:
- tokens: bfloat16 [2048, 1024], P(('expert', 'replica')), may hold values from -6 to 6
- route_ids: int32 [2048, 6], P(('expert', 'replica')), may hold values from 0 to 15, all different within a row; in each aligned block of 64 rows (0 to 63, 64 to 127, ...) at most 28 rows name the same one
- route_weights: bfloat16 [2048, 6], P(('expert', 'replica')), may hold values from 0.049804688 to 0.5
- out_grad: bfloat16 [2048, 1024], P(('expert', 'replica')), may hold values from -3 to 3
- w_gate: bfloat16 [16, 1024, 384], P('expert'), may hold values from -0.1875 to 0.1875
- w_up: bfloat16 [16, 1024, 384], P('expert'), may hold values from -0.1875 to 0.1875
- w_down: bfloat16 [16, 1024, 384], P('expert'), may hold values from -0.3125 to 0.3125
- mom_gate: float32 [16, 1024, 384], P('expert', 'replica'), may hold values from -6 to 6
- mom_up: float32 [16, 1024, 384], P('expert', 'replica'), may hold values from -6 to 6
- mom_down: float32 [16, 1024, 384], P('expert', 'replica'), may hold values from -6 to 6
Outputs:
- grad_tokens: bfloat16 [2048, 1024], P(('expert', 'replica'))
- grad_route: bfloat16 [2048, 6], P(('expert', 'replica'))
- new_gate: float32 [16, 1024, 384], P('expert', 'replica')
- new_up: float32 [16, 1024, 384], P('expert', 'replica')
- new_down: float32 [16, 1024, 384], P('expert', 'replica')
The draws below stay inside these ranges and needn't reach their ends.
Inputs may be any that keep to these rules, and one draw needn't show every extreme that they name: `route_ids`: each row names 6 different experts. Among the 64 rows of one device no expert is named more than 28 times, a bound that some block reaches.
All inputs are finite; a program needn't handle non-finite values.
Results may differ from the reference program's by a relative error of at most 0.015.
Values may be sent and summed in bfloat16 or wider, within the bound.
No kernel may reach another device: no remote copies, remote signals or barrier semaphores. Data moves between devices by JAX's collectives and lax.ppermute only.
A program may use at most 64 MiB of HBM per device.

```python
import math
import jax
import jax.numpy as jnp
import numpy as np
from jax import lax

D = 1024
FF = 384
TOPK = 6
EXP_DEV = 1
TOK_DEV = 64
EXPERTS = 16
CAP = 28
TOKENS = 2048
N_EXPERT = 16
N_REPLICA = 2


def steps_of(own_key, extent, pieces, least, top_value):
    gain, own = 1.0, jax.random.fold_in(own_key, 6)
    for dim, blocks in pieces:
        draws = jnp.exp(jax.random.uniform(jax.random.fold_in(own, dim), (blocks,), jnp.float32, least / len(pieces), top_value / len(pieces)))
        gain = gain * jnp.repeat(draws, extent[dim] // blocks).reshape([-1 if axis == dim else 1 for axis in range(len(extent))])
    return gain


def deal_out(key, own, number, rows, count, top, limit, slope):
    ranking = jax.random.permutation(key, count)
    packed, usual = portions_of(count, rows * top, limit, slope, True), portions_of(count, rows * top, limit, slope, False)
    places = jnp.arange(count)

    def named(tallies, rotation):
        used = int((tallies > 0).sum())
        fixed = max(1, used // 4)
        moved = fixed + (places - fixed + rotation * (used - fixed)) % max(1, count - fixed)
        return jnp.zeros((count,), jnp.int32).at[ranking[jnp.where(places < fixed, places, moved)]].set(jnp.asarray(tallies, jnp.int32))

    tallies = jnp.where(number % 4 == 0, named(packed, number // 4), named(usual, number - number // 4 - 1))
    mixed = jax.random.permutation(jax.random.fold_in(own, 3), count)
    donor, receiver = mixed[0:count // 2 * 2:2], mixed[1:count // 2 * 2:2]
    margin = jnp.minimum(tallies[donor] - 1, limit - tallies[receiver]) // 2
    margin = jnp.where((donor == ranking[0]) | (receiver == ranking[0]) | (tallies[receiver] == 0), 0, jnp.maximum(margin, 0))
    moved = jax.random.randint(jax.random.fold_in(own, 4), (count // 2,), 0, 1 << 20) % (margin + 1)
    tallies = tallies.at[donor].add(-moved).at[receiver].add(moved)
    labels = jnp.searchsorted(jnp.cumsum(tallies), jnp.arange(rows * top), side="right").astype(jnp.int32)
    table = labels.reshape(top, rows).T
    table = table[jax.random.permutation(jax.random.fold_in(own, 1), rows)]
    rotation = jax.random.randint(jax.random.fold_in(own, 2), (rows, 1), 0, top)
    return jnp.take_along_axis(table, (jnp.arange(top)[None, :] + rotation) % top, axis=1)


def portions_of(amount, total, most, slope, full):
    weights = [(1 << 20) // math.isqrt(standing ** slope) + 1 for standing in range(1, amount + 1)]
    largest = most if full else min(most, max(-(-total // amount), total * weights[0] // sum(weights)))
    least = 1 if total - largest >= amount - 1 else 0
    given, surplus = [largest] + [least] * (amount - 1), total - largest - least * (amount - 1)
    while surplus > 0:
        movable = [i for i in range(1, amount) if given[i] < largest] or [i for i in range(1, amount) if given[i] < most]
        mass, budget = sum([weights[i] for i in movable]), surplus
        for i in movable:
            addition = min(most - given[i], max(1, budget * weights[i] // mass), surplus)
            given[i] = given[i] + addition
            surplus = surplus - addition
    return np.array(given)


def normal_values(stream_key, extent, width, bound, shards=(), kind=jnp.bfloat16):
    entries = width * jax.random.normal(stream_key, extent, jnp.float32)
    if shards:
        entries = entries * steps_of(stream_key, extent, shards, -0.22, 0.18)
    return jnp.clip(entries, -bound, bound).astype(kind)


def setup_inputs(seed: int = 0) -> dict:
    arg_keys = jax.random.split(jax.random.key(seed), 11)
    tokens = normal_values(arg_keys[0], (TOKENS, D), 1.0, 6.0, ((0, 32),))
    route_ids_keys = jax.random.split(jax.random.fold_in(arg_keys[1], 1), TOKENS // TOK_DEV)
    route_ids_turns = jax.random.permutation(jax.random.fold_in(arg_keys[1], 3), TOKENS // TOK_DEV)
    route_ids = jax.vmap(lambda own, number: deal_out(jax.random.fold_in(arg_keys[1], 2), own, number, TOK_DEV, EXPERTS, TOPK, CAP, 2))(route_ids_keys, route_ids_turns).reshape((TOKENS, TOPK))
    route_weights = jnp.clip(jnp.exp(math.log(0.5) - 2.306499 * jax.random.uniform(arg_keys[2], (TOKENS, TOPK), jnp.float32) ** steps_of(arg_keys[2], (TOKENS, TOPK), ((0, 32),), -0.2, 0.2)), 0.049804688, 0.5).astype(jnp.bfloat16)
    out_grad = normal_values(arg_keys[3], (TOKENS, D), 0.5, 3.0, ((0, 32),))
    w_gate = normal_values(arg_keys[4], (EXPERTS, D, FF), D ** -0.5, 0.1875, ((0, 16),))
    w_up = normal_values(arg_keys[5], (EXPERTS, D, FF), D ** -0.5, 0.1875, ((0, 16),))
    w_down = normal_values(arg_keys[6], (EXPERTS, D, FF), FF ** -0.5, 0.3125, ((0, 16),))
    mom_gate = normal_values(arg_keys[7], (EXPERTS, D, FF), 1.0, 6.0, ((0, 16), (1, 2)), jnp.float32)
    mom_up = normal_values(arg_keys[8], (EXPERTS, D, FF), 1.0, 6.0, ((0, 16), (1, 2)), jnp.float32)
    mom_down = normal_values(arg_keys[9], (EXPERTS, D, FF), 1.0, 6.0, ((0, 16), (1, 2)), jnp.float32)
    return {"tokens": tokens, "route_ids": route_ids, "route_weights": route_weights, "out_grad": out_grad, "w_gate": w_gate, "w_up": w_up, "w_down": w_down, "mom_gate": mom_gate, "mom_up": mom_up, "mom_down": mom_down}


def slot_table(ids, experts, cap):
    flat = ids.reshape(-1)
    onehot = (flat[:, None] == jnp.arange(experts, dtype=jnp.int32)[None, :]).astype(jnp.int32)
    before = jnp.cumsum(onehot, axis=0) - onehot
    position = jnp.sum(before * onehot, axis=1).astype(jnp.int32)
    return flat * cap + position


def expert_step(args):
    rows, grads, weights, gate_w, up_w, down_w = args
    gate_act = jnp.dot(rows, gate_w, preferred_element_type=jnp.float32)
    up_act = jnp.dot(rows, up_w, preferred_element_type=jnp.float32)
    sig = 1.0 / (1.0 + jnp.exp(-gate_act))
    act = gate_act * sig
    hidden = act * up_act
    back = jnp.dot(grads, down_w, preferred_element_type=jnp.float32)
    route_grad = jnp.sum(hidden * back, axis=1).astype(jnp.bfloat16)
    scale = weights.astype(jnp.float32)[:, None]
    gh = scale * back
    grad_gate = (gh * up_act * sig * (1.0 + gate_act * (1.0 - sig))).astype(jnp.bfloat16)
    grad_up = (gh * act).astype(jnp.bfloat16)
    dims = (((1,), (1,)), ((), ()))
    slot_grad = lax.dot_general(grad_gate, gate_w, dims, preferred_element_type=jnp.float32)
    slot_grad = (slot_grad + lax.dot_general(grad_up, up_w, dims, preferred_element_type=jnp.float32)).astype(jnp.bfloat16)
    scaled = (scale * grads.astype(jnp.float32)).astype(jnp.bfloat16)
    hidden_b = hidden.astype(jnp.bfloat16)
    rdims = (((0,), (0,)), ((), ()))
    part_gate = lax.dot_general(rows, grad_gate, rdims, preferred_element_type=jnp.float32)
    part_up = lax.dot_general(rows, grad_up, rdims, preferred_element_type=jnp.float32)
    part_down = lax.dot_general(scaled, hidden_b, rdims, preferred_element_type=jnp.float32)
    return slot_grad, route_grad, jnp.concatenate([part_gate, part_up, part_down], axis=1)


def reference(tokens, route_ids, route_weights, out_grad, w_gate, w_up, w_down, mom_gate, mom_up, mom_down):
    experts = EXP_DEV * N_EXPERT
    cap = (7 * TOK_DEV * TOPK) // (6 * experts)
    depth = N_EXPERT * cap
    routes = TOK_DEV * TOPK

    def blocks(array):
        return array.reshape((N_EXPERT, N_REPLICA, TOK_DEV) + array.shape[1:])

    tok_blocks = blocks(tokens)
    id_blocks = blocks(route_ids)
    weight_blocks = blocks(route_weights)
    grad_blocks = blocks(out_grad)
    token_of = jnp.arange(routes, dtype=jnp.int32) // TOPK
    total = jnp.zeros((experts, D, 3 * FF), jnp.float32)
    tok_list = []
    route_list = []
    for replica_index in range(N_REPLICA):
        ids = id_blocks[:, replica_index]
        slots = jax.vmap(lambda item: slot_table(item, experts, cap))(ids)
        expert_of = ids.reshape(N_EXPERT, routes).astype(jnp.int32)
        position = slots - expert_of * cap
        row_of = (jnp.arange(N_EXPERT, dtype=jnp.int32)[:, None] * cap + position).astype(jnp.int32)
        rows = tok_blocks[:, replica_index][:, token_of]
        grads = grad_blocks[:, replica_index][:, token_of]
        weights = weight_blocks[:, replica_index].reshape(N_EXPERT, routes)
        buf_rows = jnp.zeros((experts, depth, D), tokens.dtype).at[expert_of, row_of].set(rows)
        buf_grads = jnp.zeros((experts, depth, D), out_grad.dtype).at[expert_of, row_of].set(grads)
        buf_weights = jnp.zeros((experts, depth), route_weights.dtype).at[expert_of, row_of].set(weights)
        slot_grad, route_grad, parts = lax.map(expert_step, (buf_rows, buf_grads, buf_weights, w_gate, w_up, w_down))
        rounded = lax.optimization_barrier(parts.astype(jnp.bfloat16))
        total = total + rounded.astype(jnp.float32)
        picked = slot_grad[expert_of, row_of].reshape(N_EXPERT, TOK_DEV, TOPK, D)
        tok_list.append(jnp.sum(picked.astype(jnp.float32), axis=2).astype(jnp.bfloat16))
        route_list.append(route_grad[expert_of, row_of].reshape(N_EXPERT, TOK_DEV, TOPK))
    grad_tokens = jnp.stack(tok_list, axis=1).reshape(N_EXPERT * N_REPLICA * TOK_DEV, D)
    grad_route = jnp.stack(route_list, axis=1).reshape(N_EXPERT * N_REPLICA * TOK_DEV, TOPK)
    new_gate = 0.9 * mom_gate + 0.1 * total[:, :, :FF]
    new_up = 0.9 * mom_up + 0.1 * total[:, :, FF:2 * FF]
    new_down = 0.9 * mom_down + 0.1 * total[:, :, 2 * FF:]
    return grad_tokens, grad_route, new_gate, new_up, new_down
```

```python
import functools

import jax
import jax.numpy as jnp
from jax import lax
from jax.experimental import pallas as pl
from jax.experimental.pallas import tpu as pltpu
from jax.sharding import PartitionSpec as P


F32 = jnp.float32
BF16 = jnp.bfloat16
ROWS_BY_ROWS = (((0,), (0,)), ((), ()))
COLS_BY_COLS = (((1,), (1,)), ((), ()))
VMEM = pl.BlockSpec(memory_space=pltpu.VMEM)
SMEM = pl.BlockSpec(memory_space=pltpu.SMEM)


def call(kernel, outs, ins, flops, name):
    nbytes = sum(x.size * x.dtype.itemsize for x in list(ins[1:]) + list(outs))
    return pl.pallas_call(
        kernel,
        out_shape=tuple(outs),
        in_specs=[SMEM] + [VMEM] * (len(ins) - 1),
        out_specs=tuple([VMEM] * len(outs)),
        cost_estimate=pl.CostEstimate(flops=flops, bytes_accessed=nbytes, transcendentals=0),
        compiler_params=pltpu.CompilerParams(vmem_limit_bytes=40 << 20),
        name=name,
    )(*ins)


def selection(key, value, chunk):
    experts, lanes = key.shape
    slot = lax.broadcasted_iota(jnp.int32, (experts, chunk, lanes), 1)
    hit = slot == key.astype(jnp.int32)[:, None, :]
    full = jnp.where(hit, jnp.broadcast_to(value[:, None, :], hit.shape), 0.0)
    return full.reshape(experts * chunk, lanes).astype(BF16)


def pack(key, value, tok, grad, chunk):
    both = jnp.concatenate([tok, grad], axis=0)
    return jnp.dot(selection(key, value, chunk), both, preferred_element_type=F32).astype(BF16)


def route_kernel(cap, chunk, where, ids, weights, tok, grad, packed, table, far):
    topk, rows = ids.shape
    experts, lanes = table.shape[1], table.shape[2]
    sub = experts // 2
    expert = lax.broadcasted_iota(jnp.int32, (experts, rows), 0)
    named = jnp.zeros((experts, rows), F32)
    weight = jnp.zeros((experts, rows), F32)
    for k in range(topk):
        hit = ids[k : k + 1, :] == expert
        named = named + jnp.where(hit, 1.0, 0.0)
        weight = weight + jnp.where(hit, weights[k : k + 1, :].astype(F32), 0.0)
    source = lax.broadcasted_iota(jnp.int32, (rows, lanes), 0)
    lane = lax.broadcasted_iota(jnp.int32, (rows, lanes), 1)
    target = jnp.where(lane >= rows, lane - rows, lane)
    earlier = jnp.where(source < target, 1.0, 0.0).astype(BF16)
    same = jnp.where(source == target, 1.0, 0.0).astype(BF16)
    named_b = named.astype(BF16)
    position = jnp.dot(named_b, earlier, preferred_element_type=F32)
    present = jnp.dot(named_b, same, preferred_element_type=F32)
    factor = jnp.dot(weight.astype(BF16), same, preferred_element_type=F32)
    second = lax.broadcasted_iota(jnp.int32, (experts, lanes), 1) >= rows
    table[0] = jnp.where(present > 0.5, position + jnp.where(second, 1.0 * cap, 0.0), -1.0)
    table[1] = jnp.where(second, factor, 1.0)
    own = pl.ds(pl.multiple_of(where[0] * sub, sub), sub)
    other = pl.ds(pl.multiple_of((1 - where[0]) * sub, sub), sub)
    far[0] = table[0, other, :]
    far[1] = table[1, other, :]
    packed[...] = pack(table[0, own, :], table[1, own, :], tok[...], grad[...], chunk)


def relay_kernel(chunk, where, far, tok, grad, packed):
    packed[...] = pack(far[0], far[1], tok[...], grad[...], chunk)


def expert_kernel(cap, chunk, where, got, w_gate, w_up, w_down, back_rows, small, sums):
    total, units = got.shape[0], w_gate.shape[1]
    width = got.shape[1]
    sub = total // chunk
    x = got[...]
    gate = jnp.dot(x, w_gate[...], preferred_element_type=F32)
    up = jnp.dot(x, w_up[...], preferred_element_type=F32)
    back = pltpu.roll(jnp.dot(x, w_down[...], preferred_element_type=F32), total - cap, 0)
    slot = lax.broadcasted_iota(jnp.int32, (sub, chunk, 128), 1).reshape(total, 128)
    first = slot[:, :1] < cap
    sig = 1.0 / (1.0 + jnp.exp(-gate))
    act = gate * sig
    hidden = jnp.where(first, act * up, 0.0)
    route = jnp.sum(hidden * back, axis=1, keepdims=True)
    grad_gate = jnp.where(first, back * up * sig * (1.0 + gate * (1.0 - sig)), 0.0)
    grad_up = jnp.where(first, back * act, 0.0)
    small[:, :units] = grad_gate.astype(BF16)
    small[:, units : 2 * units] = grad_up.astype(BF16)
    small[:, 2 * units :] = pltpu.roll(hidden, cap, 0).astype(BF16)
    twice_gate = (grad_gate + pltpu.roll(grad_gate, cap, 0)).astype(BF16)
    twice_up = (grad_up + pltpu.roll(grad_up, cap, 0)).astype(BF16)
    half = width // 2
    parts = []
    for i in range(2):
        rows = slice(i * half, (i + 1) * half)
        part = lax.dot_general(twice_gate, w_gate[rows, :], COLS_BY_COLS, preferred_element_type=F32)
        part = part + lax.dot_general(
            twice_up, w_up[rows, :], COLS_BY_COLS, preferred_element_type=F32
        )
        parts.append(part)
    back_rows[...] = jnp.where(first, parts[0], parts[1]).astype(BF16)
    lane = lax.broadcasted_iota(jnp.int32, (total, 128), 1)
    spread = jnp.where(lane == slot, route, 0.0).reshape(sub, chunk, 128)
    sums[...] = jnp.sum(spread, axis=1)


def weight_kernel(where, rows_a, small_a, rows_b, small_b, out):
    replicas, width = out.shape[0], out.shape[1]
    for b in range(replicas):
        cols = slice(b * width, (b + 1) * width)
        part = lax.dot_general(
            rows_a[:, cols], small_a[...], ROWS_BY_ROWS, preferred_element_type=F32
        )
        part = part + lax.dot_general(
            rows_b[:, cols], small_b[...], ROWS_BY_ROWS, preferred_element_type=F32
        )
        out[lax.rem(b - where[1] + replicas, replicas)] = part.astype(BF16)


def gathered(key, returned, chunk):
    ones = jnp.ones(key.shape, F32)
    return lax.dot_general(
        selection(key, ones, chunk), returned, ROWS_BY_ROWS, preferred_element_type=F32
    )


def partial_kernel(chunk, where, far, returned, out):
    rows, half = out.shape[0], returned.shape[1]
    total = gathered(far[0], returned[...], chunk)
    out[:, :half] = total[:rows].astype(BF16)
    out[:, half:] = total[rows:].astype(BF16)


def final_kernel(
    cap, chunk, where, table, returned, partial, sums, ids, weights, out, route
):
    rows, half = out.shape[0], returned.shape[1]
    topk = ids.shape[0]
    experts = table.shape[1]
    sub = experts // 2
    own = pl.ds(pl.multiple_of(where[0] * sub, sub), sub)
    total = gathered(table[0, own, :], returned[...], chunk)
    out[:, :half] = (total[:rows] + partial[:, :half].astype(F32)).astype(BF16)
    out[:, half:] = (total[rows:] + partial[:, half:].astype(F32)).astype(BF16)
    key = table[0].astype(jnp.int32)
    value = jnp.zeros(key.shape, F32)
    per_slot = sums[:, 0, :]
    for q in range(cap):
        value = value + jnp.where(key == q, per_slot[:, q : q + 1], 0.0)
    value = value[:, :rows]
    expert = lax.broadcasted_iota(jnp.int32, (experts, rows), 0)
    for k in range(topk):
        picked = jnp.sum(
            jnp.where(ids[k : k + 1, :] == expert, value, 0.0), axis=0, keepdims=True
        )
        route[k : k + 1, :] = (picked / weights[k : k + 1, :].astype(F32)).astype(BF16)


def per_device(
    tokens, route_ids, route_weights, out_grad, w_gate, w_up, w_down, mom_gate, mom_up, mom_down
):
    experts = lax.axis_size("expert")
    replicas = lax.axis_size("replica")
    rows, width = tokens.shape
    topk = route_ids.shape[1]
    units = w_gate.shape[2]
    cap = 7 * rows * topk // (6 * experts)
    sub = experts // 2
    chunk = -(-2 * cap // 8) * 8
    total = sub * chunk
    lanes = 2 * rows
    half = width // 2
    place = lax.axis_index("expert") // sub
    where = jnp.stack([place, lax.axis_index("replica")]).astype(jnp.int32)
    groups = [list(range(sub)), list(range(sub, experts))]
    S = jax.ShapeDtypeStruct

    def across(x):
        return lax.ppermute(x, "expert", [(i, (i + sub) % experts) for i in range(experts)])

    def within(x):
        return lax.all_to_all(
            x, "expert", split_axis=0, concat_axis=0, tiled=True, axis_index_groups=groups
        )

    ids = route_ids.T
    weights = route_weights.T
    far_tok = across(tokens)
    far_grad = across(out_grad)
    packed, table, far = call(
        functools.partial(route_kernel, cap, chunk),
        [S((total, width), BF16), S((2, experts, lanes), F32), S((2, sub, lanes), F32)],
        (where, ids, weights, tokens, out_grad),
        2 * total * lanes * width,
        "route",
    )
    far = across(far)
    got_a = within(packed)
    (relayed,) = call(
        functools.partial(relay_kernel, chunk),
        [S((total, width), BF16)],
        (where, far, far_tok, far_grad),
        2 * total * lanes * width,
        "relay",
    )
    got_b = within(relayed)

    def expert(got, name):
        return call(
            functools.partial(expert_kernel, cap, chunk),
            [S((total, half), BF16), S((total, 3 * units), BF16), S((sub, 128), F32)],
            (where, got, w_gate[0], w_up[0], w_down[0]),
            10 * total * width * units,
            name,
        )

    back_a, small_a, sums_a = expert(got_a, "expert_a")
    back_b, small_b, sums_b = expert(got_b, "expert_b")
    ret_b = within(back_b)
    ret_a = within(back_a)
    sums = jnp.where(
        place == 0,
        jnp.concatenate([sums_a, sums_b], axis=0),
        jnp.concatenate([sums_b, sums_a], axis=0),
    )
    sums = jnp.broadcast_to(sums[:, None, :], (experts, 8, 128))
    sums = lax.all_to_all(sums, "expert", split_axis=0, concat_axis=0, tiled=True)
    (partial,) = call(
        functools.partial(partial_kernel, chunk),
        [S((rows, width), BF16)],
        (where, far, ret_b),
        2 * total * lanes * half,
        "partial",
    )
    partial = across(partial)
    grad_tokens, grad_route = call(
        functools.partial(final_kernel, cap, chunk),
        [S((rows, width), BF16), S((topk, rows), BF16)],
        (where, table, ret_a, partial, sums, ids, weights),
        2 * total * lanes * half,
        "final",
    )
    (parts,) = call(
        weight_kernel,
        [S((replicas, width // replicas, 3 * units), BF16)],
        (where, got_a, small_a, got_b, small_b),
        4 * total * width * 3 * units,
        "weight",
    )
    grad_w = parts[0].astype(F32)
    for s in range(1, replicas):
        moved = lax.ppermute(
            parts[s], "replica", [(i, (i + s) % replicas) for i in range(replicas)]
        )
        grad_w = grad_w + moved.astype(F32)
    new = [
        0.9 * mom + 0.1 * grad_w[None, :, i * units : (i + 1) * units]
        for i, mom in enumerate((mom_gate, mom_up, mom_down))
    ]
    return (grad_tokens, grad_route.T, *new)


def solution(mesh):
    tok = P(("expert", "replica"), None)
    full = P("expert", None, None)
    shard = P("expert", "replica", None)
    return jax.shard_map(
        per_device,
        mesh=mesh,
        in_specs=(tok,) * 4 + (full,) * 3 + (shard,) * 3,
        out_specs=(tok, tok, shard, shard, shard),
        check_vma=False,
    )
```

```python
import functools

import jax
import jax.numpy as jnp
from jax import lax
from jax.experimental import pallas as pl
from jax.experimental.pallas import tpu as pltpu
from jax.sharding import PartitionSpec as P


F32 = jnp.float32
BF16 = jnp.bfloat16
ROWS_BY_ROWS = (((0,), (0,)), ((), ()))
COLS_BY_COLS = (((1,), (1,)), ((), ()))
VMEM = pl.BlockSpec(memory_space=pltpu.VMEM)
SMEM = pl.BlockSpec(memory_space=pltpu.SMEM)


ANY = pl.BlockSpec(memory_space=pl.ANY)


def call(kernel, outs, ins, flops, scratch=(), streamed=(), out_streamed=(), limit=32):
    nbytes = sum(x.size * x.dtype.itemsize for x in list(ins[1:]) + list(outs))
    return pl.pallas_call(
        kernel,
        out_shape=tuple(outs),
        in_specs=[SMEM] + [ANY if i in streamed else VMEM for i in range(1, len(ins))],
        out_specs=tuple(ANY if i in out_streamed else VMEM for i in range(len(outs))),
        scratch_shapes=list(scratch),
        cost_estimate=pl.CostEstimate(flops=flops, bytes_accessed=nbytes, transcendentals=0),
        compiler_params=pltpu.CompilerParams(vmem_limit_bytes=limit << 20),
    )(*ins)


class Layout:
    def __init__(self, cap):
        self.cap = cap
        self.whole = cap // 8 * 8
        self.rest = cap - self.whole
        self.mixed = -(-2 * self.rest // 8) * 8
        self.rows = 2 * self.whole + self.mixed
        self.side = self.whole + self.mixed

    def row(self, slot, second):
        late = slot >= self.whole
        first_row = slot + jnp.where(late, 1.0 * self.whole, 0.0)
        second_row = slot + jnp.where(late, 1.0 * (self.whole + self.rest), 1.0 * self.whole)
        return jnp.where(second, second_row, first_row)


def selection(key, value, chunk):
    experts, lanes = key.shape
    slot = lax.broadcasted_iota(jnp.int32, (experts, chunk, lanes), 1)
    hit = slot == key.astype(jnp.int32)[:, None, :]
    full = jnp.where(hit, jnp.broadcast_to(value[:, None, :], hit.shape), 0.0)
    return full.reshape(experts * chunk, lanes).astype(BF16)


def pack(key, value, both, chunk, staged, packed, sems):
    copies = []
    for e in range(key.shape[0]):
        pick = selection(key[e : e + 1], value[e : e + 1], chunk)
        staged[e] = jnp.dot(pick, both, preferred_element_type=F32).astype(BF16)
        copies.append(pltpu.make_async_copy(staged.at[e], packed.at[e], sems.at[e]))
        copies[-1].start()
    for copy in copies:
        copy.wait()


def route_kernel(
    lay, where, ids_in, weights_in, tok, grad, packed, table, far,
    ids, weights, both, staged, in_sems, sems,
):
    rows = tok.shape[0]
    loads = [
        pltpu.make_async_copy(ids_in, ids, in_sems.at[0]),
        pltpu.make_async_copy(weights_in, weights, in_sems.at[1]),
        pltpu.make_async_copy(tok, both.at[pl.ds(0, rows)], in_sems.at[2]),
        pltpu.make_async_copy(grad, both.at[pl.ds(rows, rows)], in_sems.at[3]),
    ]
    for load in loads:
        load.start()
    topk = ids.shape[0]
    experts, lanes = table.shape[1], table.shape[2]
    sub = experts // 2
    source = lax.broadcasted_iota(jnp.int32, (rows, lanes), 0)
    lane = lax.broadcasted_iota(jnp.int32, (rows, lanes), 1)
    target = jnp.where(lane >= rows, lane - rows, lane)
    earlier = jnp.where(source < target, 1.0, 0.0).astype(BF16)
    same = jnp.where(source == target, 1.0, 0.0).astype(BF16)
    expert = lax.broadcasted_iota(jnp.int32, (experts, rows), 0)
    named = jnp.zeros((experts, rows), F32)
    weight = jnp.zeros((experts, rows), F32)
    loads[0].wait()
    loads[1].wait()
    for k in range(topk):
        hit = ids[k : k + 1, :] == expert
        named = named + jnp.where(hit, 1.0, 0.0)
        weight = weight + jnp.where(hit, weights[k : k + 1, :].astype(F32), 0.0)
    named_b = named.astype(BF16)
    position = jnp.dot(named_b, earlier, preferred_element_type=F32)
    present = jnp.dot(named_b, same, preferred_element_type=F32)
    factor = jnp.dot(weight.astype(BF16), same, preferred_element_type=F32)
    second = lax.broadcasted_iota(jnp.int32, (experts, lanes), 1) >= rows
    table[0] = jnp.where(present > 0.5, lay.row(position, second), -1.0)
    table[1] = jnp.where(second, factor, 1.0)
    own = pl.ds(pl.multiple_of(where[0] * sub, sub), sub)
    other = pl.ds(pl.multiple_of((1 - where[0]) * sub, sub), sub)
    far[0] = table[0, other, :]
    far[1] = table[1, other, :]
    loads[2].wait()
    loads[3].wait()
    pack(table[0, own, :], table[1, own, :], both[...], lay.rows, staged, packed, sems)


def relay_kernel(lay, where, far, tok, grad, packed, staged, sems):
    both = jnp.concatenate([tok[...], grad[...]], axis=0)
    pack(far[0], far[1], both, lay.rows, staged, packed, sems)


def split_sides(lay, got, first, second):
    for e in range(got.shape[0]):
        at, side, whole = e * lay.side, lay.side, lay.whole
        if whole:
            first[at : at + whole] = got[e, :whole]
            second[at : at + whole] = got[e, whole : 2 * whole]
        first[at + whole : at + side] = got[e, 2 * whole :]
        second[at + whole : at + side] = got[e, 2 * whole :]


def align(lay, x, experts):
    parts = []
    for e in range(experts):
        at = e * lay.side
        if lay.whole:
            parts.append(x[at : at + lay.whole])
        late = x[at + lay.whole : at + lay.side]
        parts.append(pltpu.roll(late, lay.mixed - lay.rest, 0) if lay.rest else late)
    return jnp.concatenate(parts, axis=0)


def expert_kernel(
    lay, where, got, gate_in, up_in, down_in, back_rows, first, second, small, down_small, sums,
    w_gate, w_up, w_down, staged, in_sems, sems,
):
    loads = [
        pltpu.make_async_copy(gate_in, w_gate, in_sems.at[0]),
        pltpu.make_async_copy(up_in, w_up, in_sems.at[1]),
        pltpu.make_async_copy(down_in, w_down, in_sems.at[2]),
    ]
    for load in loads:
        load.start()
    sub, _, width = got.shape
    units = w_gate.shape[1]
    total = sub * lay.side
    split_sides(lay, got, first, second)
    loads[0].wait()
    gate = jnp.dot(first[...], w_gate[...], preferred_element_type=F32)
    loads[1].wait()
    up = jnp.dot(first[...], w_up[...], preferred_element_type=F32)
    loads[2].wait()
    back = jnp.dot(second[...], w_down[...], preferred_element_type=F32)
    back = align(lay, back, sub)
    slot = lax.broadcasted_iota(jnp.int32, (sub, lay.side, 128), 1).reshape(total, 128)
    filled = slot[:, :1] < lay.cap
    sig = 1.0 / (1.0 + jnp.exp(-gate))
    act = gate * sig
    hidden = jnp.where(filled, act * up, 0.0)
    grad_gate = jnp.where(filled, back * up * sig * (1.0 + gate * (1.0 - sig)), 0.0).astype(BF16)
    grad_up = jnp.where(filled, back * act, 0.0).astype(BF16)
    slot_grad = lax.dot_general(grad_gate, w_gate[...], COLS_BY_COLS, preferred_element_type=F32)
    slot_grad = slot_grad + lax.dot_general(
        grad_up, w_up[...], COLS_BY_COLS, preferred_element_type=F32
    )
    half = width // 2
    copies = []
    early = lax.broadcasted_iota(jnp.int32, (lay.mixed, half), 0) < lay.rest
    for e in range(sub):
        at, whole = e * lay.side, lay.whole
        if whole:
            staged[e, :whole] = slot_grad[at : at + whole, :half].astype(BF16)
            staged[e, whole : 2 * whole] = slot_grad[at : at + whole, half:].astype(BF16)
        late = slot_grad[at + whole : at + lay.side]
        if lay.rest:
            mixed = jnp.where(early, late[:, :half], pltpu.roll(late[:, half:], lay.rest, 0))
            staged[e, 2 * whole :] = mixed.astype(BF16)
        copies.append(pltpu.make_async_copy(staged.at[e], back_rows.at[e], sems.at[e]))
        copies[-1].start()
    small[:, :units] = grad_gate
    small[:, units:] = grad_up
    parts = []
    for e in range(sub):
        at, whole = e * lay.side, lay.whole
        if whole:
            parts.append(hidden[at : at + whole])
        late = hidden[at + whole : at + lay.side]
        parts.append(pltpu.roll(late, lay.rest, 0) if lay.rest else late)
    down_small[...] = jnp.concatenate(parts, axis=0).astype(BF16)
    route = jnp.sum(hidden * back, axis=1, keepdims=True)
    lane = lax.broadcasted_iota(jnp.int32, (total, 128), 1)
    spread = jnp.where(lane == slot, route, 0.0).reshape(sub, lay.side, 128)
    sums[...] = jnp.sum(spread, axis=1)
    for copy in copies:
        copy.wait()


def weight_parts(where, first, second, small, down_small, turned, replicas):
    width = first.shape[1] // replicas
    for b in range(replicas):
        turned[0, b] = first[:, b * width : (b + 1) * width]
        turned[1, b] = second[:, b * width : (b + 1) * width]
    for s in range(replicas):
        b = lax.rem(where[1] + s, replicas)
        upper = lax.dot_general(
            turned[0, b], small[...], ROWS_BY_ROWS, preferred_element_type=F32
        )
        lower = lax.dot_general(
            turned[1, b], down_small[...], ROWS_BY_ROWS, preferred_element_type=F32
        )
        yield s, upper, lower


def weight_a_kernel(where, first, second, small, down_small, out, turned):
    columns = small.shape[1]
    for s, upper, lower in weight_parts(
        where, first, second, small, down_small, turned, out.shape[0]
    ):
        out[s, :, :columns] = upper
        out[s, :, columns:] = lower


def weight_b_kernel(replicas, where, first, second, small, down_small, part, *rest):
    outs, turned = rest[:replicas], rest[replicas]
    columns = small.shape[1]
    for s, upper, lower in weight_parts(
        where, first, second, small, down_small, turned, replicas
    ):
        outs[s][:, :columns] = (part[s, :, :columns] + upper).astype(BF16)
        outs[s][:, columns:] = (part[s, :, columns:] + lower).astype(BF16)


def update_kernel(replicas, *refs):
    parts, moms, outs = refs[:replicas], refs[replicas : replicas + 3], refs[replicas + 3 :]
    units = moms[0].shape[2]
    for i in range(3):
        cols = slice(i * units, (i + 1) * units)
        total = parts[0][:, cols].astype(F32)
        for part in parts[1:]:
            total = total + part[:, cols].astype(F32)
        outs[i][0] = 0.9 * moms[i][0] + 0.1 * total


def gathered(key, returned, chunk):
    ones = jnp.ones(key.shape, F32)
    flat = returned.reshape(returned.shape[0] * returned.shape[1], returned.shape[2])
    return lax.dot_general(
        selection(key, ones, chunk), flat, ROWS_BY_ROWS, preferred_element_type=F32
    )


def partial_kernel(lay, where, far, returned, out):
    rows, half = out.shape[0], returned.shape[2]
    total = gathered(far[0], returned[...], lay.rows)
    out[:, :half] = total[:rows].astype(BF16)
    out[:, half:] = total[rows:].astype(BF16)


def final_kernel(lay, where, table, returned, partial, sums, ids, weights, out, route):
    rows, half = out.shape[0], returned.shape[2]
    topk = ids.shape[0]
    experts = table.shape[1]
    sub = experts // 2
    own = pl.ds(pl.multiple_of(where[0] * sub, sub), sub)
    total = gathered(table[0, own, :], returned[...], lay.rows)
    out[:, :half] = (total[:rows] + partial[:, :half].astype(F32)).astype(BF16)
    out[:, half:] = (total[rows:] + partial[:, half:].astype(F32)).astype(BF16)
    key = table[0]
    key = jnp.where(key >= lay.whole, key - lay.whole, key).astype(jnp.int32)
    value = jnp.zeros(key.shape, F32)
    per_slot = sums[:, 0, :]
    for q in range(lay.cap):
        value = value + jnp.where(key == q, per_slot[:, q : q + 1], 0.0)
    value = value[:, :rows]
    expert = lax.broadcasted_iota(jnp.int32, (experts, rows), 0)
    for k in range(topk):
        picked = jnp.sum(
            jnp.where(ids[k : k + 1, :] == expert, value, 0.0), axis=0, keepdims=True
        )
        route[k : k + 1, :] = (picked / weights[k : k + 1, :].astype(F32)).astype(BF16)


def per_device(
    tokens, route_ids, route_weights, out_grad, w_gate, w_up, w_down, mom_gate, mom_up, mom_down
):
    experts = lax.axis_size("expert")
    replicas = lax.axis_size("replica")
    rows, width = tokens.shape
    topk = route_ids.shape[1]
    units = w_gate.shape[2]
    lay = Layout(7 * rows * topk // (6 * experts))
    sub = experts // 2
    lanes = 2 * rows
    half = width // 2
    strip = width // replicas
    total = sub * lay.side
    place = lax.axis_index("expert") // sub
    where = jnp.stack([place, lax.axis_index("replica")]).astype(jnp.int32)
    groups = [list(range(sub)), list(range(sub, experts))]
    S = jax.ShapeDtypeStruct
    DMA = pltpu.SemaphoreType.DMA

    def across(x):
        return lax.ppermute(
            x, "expert", [(i, (i + sub) % experts) for i in range(experts)]
        )

    def within(x):
        return lax.all_to_all(
            x, "expert", split_axis=0, concat_axis=0, tiled=True, axis_index_groups=groups
        )

    ids = route_ids.T
    weights = route_weights.T
    far_tok = across(tokens)
    far_grad = across(out_grad)
    chunks = S((sub, lay.rows, width), BF16)
    staged = pltpu.VMEM(chunks.shape, BF16)
    packed, table, far = call(
        functools.partial(route_kernel, lay),
        [chunks, S((2, experts, lanes), F32), S((2, sub, lanes), F32)],
        (where, ids, weights, tokens, out_grad),
        2 * sub * lay.rows * lanes * width,
        scratch=[
            pltpu.VMEM(ids.shape, ids.dtype),
            pltpu.VMEM(weights.shape, weights.dtype),
            pltpu.VMEM((2 * rows, width), BF16),
            staged,
            DMA((4,)),
            DMA((sub,)),
        ],
        streamed=(1, 2, 3, 4),
        out_streamed=(0,),
        limit=16,
    )
    far = across(far)
    got_a = within(packed)
    (relayed,) = call(
        functools.partial(relay_kernel, lay),
        [chunks],
        (where, far, far_tok, far_grad),
        2 * sub * lay.rows * lanes * width,
        scratch=[staged, DMA((sub,))],
        out_streamed=(0,),
        limit=16,
    )
    got_b = within(relayed)

    def expert(got):
        weight = pltpu.VMEM((width, units), BF16)
        return call(
            functools.partial(expert_kernel, lay),
            [
                S((sub, lay.rows, half), BF16),
                S((total, width), BF16),
                S((total, width), BF16),
                S((total, 2 * units), BF16),
                S((total, units), BF16),
                S((sub, 128), F32),
            ],
            (where, got, w_gate[0], w_up[0], w_down[0]),
            10 * total * width * units,
            scratch=[weight, weight, weight, pltpu.VMEM((sub, lay.rows, half), BF16)]
            + [DMA((3,)), DMA((sub,))],
            streamed=(2, 3, 4),
            out_streamed=(0,),
        )

    back_a, *factors_a, sums_a = expert(got_a)
    turned = pltpu.VMEM((2, replicas, total, strip), BF16)
    (part_a,) = call(
        weight_a_kernel,
        [S((replicas, strip, 3 * units), F32)],
        (where, *factors_a),
        6 * total * width * units,
        scratch=[turned],
    )
    back_b, *factors_b, sums_b = expert(got_b)
    ret_b = within(back_b)
    ret_a = within(back_a)
    parts = call(
        functools.partial(weight_b_kernel, replicas),
        [S((strip, 3 * units), BF16)] * replicas,
        (where, *factors_b, part_a),
        6 * total * width * units,
        scratch=[turned],
    )
    moved = [
        lax.ppermute(
            parts[s], "replica", [(i, (i + s) % replicas) for i in range(replicas)]
        )
        for s in range(1, replicas)
    ]
    (partial,) = call(
        functools.partial(partial_kernel, lay),
        [S((rows, width), BF16)],
        (where, far, ret_b),
        2 * sub * lay.rows * lanes * half,
        limit=16,
    )
    partial = across(partial)
    sums = jnp.where(
        place == 0,
        jnp.concatenate([sums_a, sums_b], axis=0),
        jnp.concatenate([sums_b, sums_a], axis=0),
    )
    sums = jnp.broadcast_to(sums[:, None, :], (experts, 8, 128))
    sums = lax.all_to_all(sums, "expert", split_axis=0, concat_axis=0, tiled=True)
    block = min(128, strip)
    mom_spec = pl.BlockSpec((1, block, units), lambda i: (0, i, 0))
    part_spec = pl.BlockSpec((block, 3 * units), lambda i: (i, 0))
    new = pl.pallas_call(
        functools.partial(update_kernel, replicas),
        grid=(strip // block,),
        out_shape=[S(mom_gate.shape, F32)] * 3,
        in_specs=[part_spec] * replicas + [mom_spec] * 3,
        out_specs=[mom_spec] * 3,
        cost_estimate=pl.CostEstimate(
            flops=9 * strip * units,
            bytes_accessed=24 * strip * units + 6 * replicas * strip * units,
            transcendentals=0,
        ),
        compiler_params=pltpu.CompilerParams(vmem_limit_bytes=16 << 20),
        name="update",
    )(parts[0], *moved, mom_gate, mom_up, mom_down)
    grad_tokens, grad_route = call(
        functools.partial(final_kernel, lay),
        [S((rows, width), BF16), S((topk, rows), BF16)],
        (where, table, ret_a, partial, sums, ids, weights),
        2 * sub * lay.rows * lanes * half,
        limit=16,
    )
    return (grad_tokens, grad_route.T, *new)


def solution(mesh):
    tok = P(("expert", "replica"), None)
    full = P("expert", None, None)
    shard = P("expert", "replica", None)
    return jax.shard_map(
        per_device,
        mesh=mesh,
        in_specs=(tok,) * 4 + (full,) * 3 + (shard,) * 3,
        out_specs=(tok, tok, shard, shard, shard),
        check_vma=False,
    )
```

```python
import functools

import jax
import jax.numpy as jnp
from jax import lax
from jax.experimental import pallas as pl
from jax.experimental.pallas import tpu as pltpu
from jax.sharding import PartitionSpec as P


F32 = jnp.float32
BF16 = jnp.bfloat16
ROWS_BY_ROWS = (((0,), (0,)), ((), ()))
COLS_BY_COLS = (((1,), (1,)), ((), ()))
VMEM = pl.BlockSpec(memory_space=pltpu.VMEM)
SMEM = pl.BlockSpec(memory_space=pltpu.SMEM)


HBM = pl.BlockSpec(memory_space=pltpu.HBM)


def call(kernel, outs, ins, flops, scratch=(), streamed=(), out_streamed=(), limit=16):
    nbytes = sum(x.size * x.dtype.itemsize for x in list(ins[1:]) + list(outs))
    ins = [
        pltpu.with_memory_space_constraint(x, pltpu.HBM) if i in streamed else x
        for i, x in enumerate(ins)
    ]
    outs = [
        pltpu.HBM(x.shape, x.dtype) if i in out_streamed else x for i, x in enumerate(outs)
    ]
    return pl.pallas_call(
        kernel,
        out_shape=tuple(outs),
        in_specs=[SMEM] + [HBM if i in streamed else VMEM for i in range(1, len(ins))],
        out_specs=tuple(HBM if i in out_streamed else VMEM for i in range(len(outs))),
        scratch_shapes=list(scratch),
        cost_estimate=pl.CostEstimate(flops=flops, bytes_accessed=nbytes, transcendentals=0),
        compiler_params=pltpu.CompilerParams(vmem_limit_bytes=limit << 20),
    )(*ins)


class Layout:
    def __init__(self, cap):
        self.cap = cap
        self.whole = cap // 8 * 8
        self.rest = cap - self.whole
        self.mixed = -(-2 * self.rest // 8) * 8
        self.rows = 2 * self.whole + self.mixed
        self.side = self.whole + self.mixed

    def row(self, slot, second):
        late = slot >= self.whole
        first_row = slot + jnp.where(late, 1.0 * self.whole, 0.0)
        second_row = slot + jnp.where(late, 1.0 * (self.whole + self.rest), 1.0 * self.whole)
        return jnp.where(second, second_row, first_row)


def selection(key, value, chunk):
    experts, lanes = key.shape
    slot = lax.broadcasted_iota(jnp.int32, (experts, chunk, lanes), 1)
    hit = slot == key.astype(jnp.int32)[:, None, :]
    full = jnp.where(hit, jnp.broadcast_to(value[:, None, :], hit.shape), 0.0)
    return full.reshape(experts * chunk, lanes).astype(BF16)


def pack(pairs, both, chunk, staged, outs, sems):
    copies = []
    for e, (key, value) in enumerate(pairs):
        pick = selection(key, value, chunk)
        staged[e] = jnp.dot(pick, both, preferred_element_type=F32).astype(BF16)
        copies.append(pltpu.make_async_copy(staged.at[e], outs[e], sems.at[e]))
        copies[-1].start()
    for copy in copies:
        copy.wait()


def route_kernel(lay, sub, where, ids_in, weights_in, tok, grad, *refs):
    packed, (table, far, ids, weights, both, staged, in_sems, sems) = refs[:sub], refs[sub:]
    rows = tok.shape[0]
    loads = [
        pltpu.make_async_copy(ids_in, ids, in_sems.at[0]),
        pltpu.make_async_copy(weights_in, weights, in_sems.at[1]),
        pltpu.make_async_copy(tok, both.at[pl.ds(0, rows)], in_sems.at[2]),
        pltpu.make_async_copy(grad, both.at[pl.ds(rows, rows)], in_sems.at[3]),
    ]
    for load in loads:
        load.start()
    topk = ids.shape[0]
    experts, lanes = table.shape[1], table.shape[2]
    source = lax.broadcasted_iota(jnp.int32, (rows, lanes), 0)
    lane = lax.broadcasted_iota(jnp.int32, (rows, lanes), 1)
    target = jnp.where(lane >= rows, lane - rows, lane)
    earlier = jnp.where(source < target, 1.0, 0.0).astype(BF16)
    same = jnp.where(source == target, 1.0, 0.0).astype(BF16)
    expert = lax.broadcasted_iota(jnp.int32, (experts, rows), 0)
    named = jnp.zeros((experts, rows), F32)
    weight = jnp.zeros((experts, rows), F32)
    loads[0].wait()
    loads[1].wait()
    for k in range(topk):
        hit = ids[k : k + 1, :] == expert
        named = named + jnp.where(hit, 1.0, 0.0)
        weight = weight + jnp.where(hit, weights[k : k + 1, :].astype(F32), 0.0)
    named_b = named.astype(BF16)
    position = jnp.dot(named_b, earlier, preferred_element_type=F32)
    present = jnp.dot(named_b, same, preferred_element_type=F32)
    factor = jnp.dot(weight.astype(BF16), same, preferred_element_type=F32)
    second = lax.broadcasted_iota(jnp.int32, (experts, lanes), 1) >= rows
    table[0] = jnp.where(present > 0.5, lay.row(position, second), -1.0)
    table[1] = jnp.where(second, factor, 1.0)
    other = pl.ds(pl.multiple_of((1 - where[0]) * sub, sub), sub)
    far[0] = table[0, other, :]
    far[1] = table[1, other, :]
    loads[2].wait()
    loads[3].wait()
    pairs = []
    for offset in range(sub):
        row = pl.ds(where[0] * sub + (where[2] ^ offset), 1)
        pairs.append((table[0, row, :], table[1, row, :]))
    pack(pairs, both[...], lay.rows, staged, packed, sems)


def relay_kernel(lay, where, far, tok, grad, packed, staged, sems):
    both = jnp.concatenate([tok[...], grad[...]], axis=0)
    sub = packed.shape[0]
    pairs = [(far[0, e : e + 1], far[1, e : e + 1]) for e in range(sub)]
    pack(pairs, both, lay.rows, staged, [packed.at[e] for e in range(sub)], sems)


def split_sides(lay, got, first, second):
    for e, chunk in enumerate(got):
        at, side, whole = e * lay.side, lay.side, lay.whole
        if whole:
            first[at : at + whole] = chunk[:whole]
            second[at : at + whole] = chunk[whole : 2 * whole]
        first[at + whole : at + side] = chunk[2 * whole :]
        second[at + whole : at + side] = chunk[2 * whole :]


def align(lay, x, experts):
    parts = []
    for e in range(experts):
        at = e * lay.side
        if lay.whole:
            parts.append(x[at : at + lay.whole])
        late = x[at + lay.whole : at + lay.side]
        parts.append(pltpu.roll(late, lay.mixed - lay.rest, 0) if lay.rest else late)
    return jnp.concatenate(parts, axis=0)


def expert_kernel(lay, sub, direct, where, *refs):
    if direct:
        got, refs = refs[:sub], refs[sub:]
    else:
        got, refs = [refs[0].at[e] for e in range(sub)], refs[1:]
    gate_in, up_in, down_in, back_rows, *kept = refs[:8]
    w_gate, w_up, w_down, staged, first, second, small, down_small = refs[8:16]
    in_sems, sems, kept_sems = refs[16:19]
    loads = [
        pltpu.make_async_copy(gate_in, w_gate, in_sems.at[0]),
        pltpu.make_async_copy(up_in, w_up, in_sems.at[1]),
        pltpu.make_async_copy(down_in, w_down, in_sems.at[2]),
    ]
    stores = [
        pltpu.make_async_copy(held, out, kept_sems.at[i])
        for i, (held, out) in enumerate(zip((first, second, small, down_small), kept))
    ]
    width, units = w_gate.shape
    total = sub * lay.side
    if direct:
        local, local_sems = refs[19:]
        arrivals = [
            pltpu.make_async_copy(got[e], local.at[e], local_sems.at[e]) for e in range(sub)
        ]
        for copy in arrivals + loads:
            copy.start()
        for copy in arrivals:
            copy.wait()
        got = [local.at[e] for e in range(sub)]
    else:
        for load in loads:
            load.start()
    split_sides(lay, got, first, second)
    stores[0].start()
    stores[1].start()
    loads[0].wait()
    gate = jnp.dot(first[...], w_gate[...], preferred_element_type=F32)
    loads[1].wait()
    up = jnp.dot(first[...], w_up[...], preferred_element_type=F32)
    loads[2].wait()
    back = jnp.dot(second[...], w_down[...], preferred_element_type=F32)
    back = align(lay, back, sub)
    slot = lax.broadcasted_iota(jnp.int32, (sub, lay.side, 128), 1).reshape(total, 128)
    filled = slot[:, :1] < lay.cap
    sig = 1.0 / (1.0 + jnp.exp(-gate))
    act = gate * sig
    hidden = jnp.where(filled, act * up, 0.0)
    grad_gate = jnp.where(filled, back * up * sig * (1.0 + gate * (1.0 - sig)), 0.0).astype(BF16)
    grad_up = jnp.where(filled, back * act, 0.0).astype(BF16)
    slot_grad = lax.dot_general(grad_gate, w_gate[...], COLS_BY_COLS, preferred_element_type=F32)
    slot_grad = slot_grad + lax.dot_general(
        grad_up, w_up[...], COLS_BY_COLS, preferred_element_type=F32
    )
    route = jnp.sum(hidden * back, axis=1, keepdims=True)
    lane = lax.broadcasted_iota(jnp.int32, (total, 128), 1)
    spread = jnp.where(lane == slot, route, 0.0).reshape(sub, lay.side, 128)
    sums = jnp.sum(spread, axis=1)
    half = width // 2
    copies = []
    early = lax.broadcasted_iota(jnp.int32, (lay.mixed, half), 0) < lay.rest
    for e in range(sub):
        at, whole = e * lay.side, lay.whole
        if whole:
            staged[e, :whole] = slot_grad[at : at + whole, :half].astype(BF16)
            staged[e, whole : 2 * whole] = slot_grad[at : at + whole, half:].astype(BF16)
        late = slot_grad[at + whole : at + lay.side]
        if lay.rest:
            mixed = jnp.where(early, late[:, :half], pltpu.roll(late[:, half:], lay.rest, 0))
            staged[e, 2 * whole : lay.rows] = mixed.astype(BF16)
        staged[e, lay.rows :, :128] = jnp.broadcast_to(sums[e : e + 1], (8, 128)).astype(BF16)
        staged[e, lay.rows :, 128:] = jnp.zeros((8, half - 128), BF16)
        target = (where[2] ^ e) if direct else e
        copies.append(pltpu.make_async_copy(staged.at[e], back_rows.at[target], sems.at[e]))
        copies[-1].start()
    small[:, :units] = grad_gate
    small[:, units:] = grad_up
    stores[2].start()
    parts = []
    for e in range(sub):
        at, whole = e * lay.side, lay.whole
        if whole:
            parts.append(hidden[at : at + whole])
        late = hidden[at + whole : at + lay.side]
        parts.append(pltpu.roll(late, lay.rest, 0) if lay.rest else late)
    down_small[...] = jnp.concatenate(parts, axis=0).astype(BF16)
    stores[3].start()
    for copy in copies + stores:
        copy.wait()


def weight_kernel(replicas, where, *refs):
    sources, outs, refs = refs[:8], refs[8 : 8 + replicas], refs[8 + replicas :]
    held, (firsts, seconds, sems) = refs[:4], refs[4:]
    first, second, small, down_small = held
    width = firsts.shape[2]
    units = down_small.shape[1]
    total = sources[0].shape[0]
    loads = []
    for i in range(8):
        rows = pl.ds((i // 4) * total, total)
        loads.append(pltpu.make_async_copy(sources[i], held[i % 4].at[rows], sems.at[i]))
        loads[-1].start()
    for load in loads:
        load.wait()
    for b in range(replicas):
        cols = slice(b * width, (b + 1) * width)
        firsts[b] = first[:, cols]
        seconds[b] = second[:, cols]
    for s in reversed(range(replicas)):
        b = lax.rem(where[1] + s, replicas)
        outs[s][:, : 2 * units] = lax.dot_general(
            firsts[b], small[...], ROWS_BY_ROWS, preferred_element_type=F32
        ).astype(BF16)
        outs[s][:, 2 * units :] = lax.dot_general(
            seconds[b], down_small[...], ROWS_BY_ROWS, preferred_element_type=F32
        ).astype(BF16)


def update_kernel(replicas, where, *refs):
    parts, moms, outs = refs[:replicas], refs[replicas : replicas + 3], refs[replicas + 3 :]
    outs, (held, made, in_sems, out_sems) = outs[:3], outs[3:]
    units = moms[0].shape[2]
    loads = [pltpu.make_async_copy(moms[i].at[0], held.at[i], in_sems.at[i]) for i in range(3)]
    stores = [pltpu.make_async_copy(made.at[i], outs[i].at[0], out_sems.at[i]) for i in range(3)]
    for load in loads:
        load.start()
    for i in range(3):
        cols = slice(i * units, (i + 1) * units)
        total = parts[0][:, cols].astype(F32)
        for part in parts[1:]:
            total = total + part[:, cols].astype(F32)
        loads[i].wait()
        made[i] = 0.9 * held[i] + 0.1 * total
        stores[i].start()
    for store in stores:
        store.wait()


def gathered(key, returned):
    ones = jnp.ones(key.shape, F32)
    chunk = returned.shape[1]
    flat = returned.reshape(returned.shape[0] * chunk, returned.shape[2])
    return lax.dot_general(
        selection(key, ones, chunk), flat, ROWS_BY_ROWS, preferred_element_type=F32
    )


def route_values(lay, key, returned):
    key = jnp.where(key >= lay.whole, key - lay.whole, key).astype(jnp.int32)
    value = jnp.zeros(key.shape, F32)
    per_slot = returned[:, lay.rows, :128].astype(F32)
    for q in range(lay.cap):
        value = value + jnp.where(key == q, per_slot[:, q : q + 1], 0.0)
    return value


def partial_kernel(lay, rows, where, far, returned, out):
    sub, _, half = returned.shape
    lanes = far.shape[2]
    total = gathered(far[0], returned[...])
    out[:rows, :half] = total[:rows].astype(BF16)
    out[:rows, half:] = total[rows:].astype(BF16)
    out[rows:, :lanes] = route_values(lay, far[0], returned[...]).astype(BF16)
    out[rows:, lanes:] = jnp.zeros((sub, 2 * half - lanes), BF16)


def final_kernel(lay, where, table, returned, partial, ids, weights, out, route):
    rows, half = out.shape[0], returned.shape[2]
    topk = ids.shape[0]
    sub = returned.shape[0]
    own = table[0, pl.ds(pl.multiple_of(where[0] * sub, sub), sub), :]
    total = gathered(own, returned[...])
    out[:, :half] = (total[:rows] + partial[:rows, :half].astype(F32)).astype(BF16)
    out[:, half:] = (total[rows:] + partial[:rows, half:].astype(F32)).astype(BF16)
    near = route_values(lay, own, returned[...])[:, :rows]
    far = partial[rows:, :rows].astype(F32)
    expert = lax.broadcasted_iota(jnp.int32, (sub, rows), 0)
    near_expert, far_expert = expert + where[0] * sub, expert + (1 - where[0]) * sub
    for k in range(topk):
        name = ids[k : k + 1, :]
        picked = jnp.where(name == near_expert, near, 0.0)
        picked = picked + jnp.where(name == far_expert, far, 0.0)
        picked = jnp.sum(picked, axis=0, keepdims=True)
        route[k : k + 1, :] = (picked / weights[k : k + 1, :].astype(F32)).astype(BF16)


def per_device(
    tokens, route_ids, route_weights, out_grad, w_gate, w_up, w_down, mom_gate, mom_up, mom_down
):
    experts = lax.axis_size("expert")
    replicas = lax.axis_size("replica")
    rows, width = tokens.shape
    topk = route_ids.shape[1]
    units = w_gate.shape[2]
    lay = Layout(7 * rows * topk // (6 * experts))
    sub = experts // 2
    lanes = 2 * rows
    half = width // 2
    strip = width // replicas
    total = sub * lay.side
    me = lax.axis_index("expert")
    place = me // sub
    where = jnp.stack([place, lax.axis_index("replica"), me % sub]).astype(jnp.int32)
    groups = [list(range(sub)), list(range(sub, experts))]
    S = jax.ShapeDtypeStruct
    DMA = pltpu.SemaphoreType.DMA

    def permute(x, partner):
        return lax.ppermute(x, "expert", [(i, partner(i)) for i in range(experts)])

    def across(x):
        return permute(x, lambda i: (i + sub) % experts)

    def within(x):
        return lax.all_to_all(
            x, "expert", split_axis=0, concat_axis=0, tiled=True, axis_index_groups=groups
        )

    ids = route_ids.T
    weights = route_weights.T
    far_tok = across(tokens)
    far_grad = across(out_grad)
    chunk = S((lay.rows, width), BF16)
    staged = pltpu.VMEM((sub, *chunk.shape), BF16)
    *packed, table, far = call(
        functools.partial(route_kernel, lay, sub),
        [chunk] * sub + [S((2, experts, lanes), F32), S((2, sub, lanes), F32)],
        (where, ids, weights, tokens, out_grad),
        2 * sub * lay.rows * lanes * width,
        scratch=[
            pltpu.VMEM(ids.shape, ids.dtype),
            pltpu.VMEM(weights.shape, weights.dtype),
            pltpu.VMEM((2 * rows, width), BF16),
            staged,
            DMA((4,)),
            DMA((sub,)),
        ],
        streamed=(1, 2, 3, 4),
        out_streamed=range(sub),
    )
    far = across(far)
    got_a = packed[:1] + [permute(packed[offset], lambda i: i ^ offset) for offset in range(1, sub)]
    (relayed,) = call(
        functools.partial(relay_kernel, lay),
        [S((sub, *chunk.shape), BF16)],
        (where, far, far_tok, far_grad),
        2 * sub * lay.rows * lanes * width,
        scratch=[staged, DMA((sub,))],
        out_streamed=(0,),
    )
    got_b = [within(relayed)]

    def expert(got, direct):
        weight = pltpu.VMEM((width, units), BF16)
        back = S((sub, lay.rows + 8, half), BF16)
        kept = [S((total, cols), BF16) for cols in (width, width, 2 * units, units)]
        local = [pltpu.VMEM((sub, *chunk.shape), BF16), DMA((sub,))]
        first_weight = len(got) + 1
        return call(
            functools.partial(expert_kernel, lay, sub, direct),
            [back] + kept,
            (where, *got, w_gate[0], w_up[0], w_down[0]),
            10 * total * width * units,
            scratch=[weight, weight, weight, pltpu.VMEM(back.shape, BF16)]
            + [pltpu.VMEM(x.shape, BF16) for x in kept]
            + [DMA((3,)), DMA((sub,)), DMA((4,))]
            + (local if direct else []),
            streamed=range(1 if direct else first_weight, first_weight + 3),
            out_streamed=range(5),
        )

    back_a, *factors_a = expert(got_a, True)
    back_b, *factors_b = expert(got_b, False)
    ret_b = within(back_b)
    turned = pltpu.VMEM((replicas, 2 * total, strip), BF16)
    parts = call(
        functools.partial(weight_kernel, replicas),
        [S((strip, 3 * units), BF16)] * replicas,
        (where, *factors_a, *factors_b),
        12 * total * width * units,
        scratch=[pltpu.VMEM((2 * x.shape[0], x.shape[1]), BF16) for x in factors_a]
        + [turned, turned, DMA((8,))],
        streamed=range(1, 9),
        limit=16 if strip >= 128 else 48,
    )
    moved = [
        lax.ppermute(
            parts[s], "replica", [(i, (i + s) % replicas) for i in range(replicas)]
        )
        for s in range(1, replicas)
    ]
    (partial,) = call(
        functools.partial(partial_kernel, lay, rows),
        [S((rows + sub, width), BF16)],
        (where, far, ret_b),
        2 * sub * lay.rows * lanes * half,
    )
    partial = across(partial)
    ret_a = within(back_a)
    new = call(
        functools.partial(update_kernel, replicas),
        [S(mom_gate.shape, F32)] * 3,
        (where, parts[0], *moved, mom_gate, mom_up, mom_down),
        9 * strip * units,
        scratch=[pltpu.VMEM((3, strip, units), F32)] * 2 + [DMA((3,)), DMA((3,))],
        streamed=range(replicas + 1, replicas + 4),
        out_streamed=range(3),
    )
    grad_tokens, grad_route = call(
        functools.partial(final_kernel, lay),
        [S((rows, width), BF16), S((topk, rows), BF16)],
        (where, table, ret_a, partial, ids, weights),
        2 * sub * lay.rows * lanes * half,
    )
    return (grad_tokens, grad_route.T, *new)


def solution(mesh):
    tok = P(("expert", "replica"), None)
    full = P("expert", None, None)
    shard = P("expert", "replica", None)
    return jax.shard_map(
        per_device,
        mesh=mesh,
        in_specs=(tok,) * 4 + (full,) * 3 + (shard,) * 3,
        out_specs=(tok, tok, shard, shard, shard),
        check_vma=False,
    )
```

```python
import functools

import jax
import jax.numpy as jnp
from jax import lax
from jax.experimental import pallas as pl
from jax.experimental.pallas import tpu as pltpu
from jax.sharding import PartitionSpec as P


F32 = jnp.float32
BF16 = jnp.bfloat16
ROWS_BY_ROWS = (((0,), (0,)), ((), ()))
COLS_BY_COLS = (((1,), (1,)), ((), ()))
VMEM = pl.BlockSpec(memory_space=pltpu.VMEM)
SMEM = pl.BlockSpec(memory_space=pltpu.SMEM)


HBM = pl.BlockSpec(memory_space=pltpu.HBM)


def call(kernel, outs, ins, flops, scratch=(), streamed=(), out_streamed=(), limit=16):
    nbytes = sum(x.size * x.dtype.itemsize for x in list(ins[1:]) + list(outs))
    ins = [
        pltpu.with_memory_space_constraint(x, pltpu.HBM) if i in streamed else x
        for i, x in enumerate(ins)
    ]
    outs = [
        pltpu.HBM(x.shape, x.dtype) if i in out_streamed else x for i, x in enumerate(outs)
    ]
    return pl.pallas_call(
        kernel,
        out_shape=tuple(outs),
        in_specs=[SMEM] + [HBM if i in streamed else VMEM for i in range(1, len(ins))],
        out_specs=tuple(HBM if i in out_streamed else VMEM for i in range(len(outs))),
        scratch_shapes=list(scratch),
        cost_estimate=pl.CostEstimate(flops=flops, bytes_accessed=nbytes, transcendentals=0),
        compiler_params=pltpu.CompilerParams(vmem_limit_bytes=limit << 20),
    )(*ins)


class Layout:
    def __init__(self, cap):
        self.cap = cap
        self.whole = cap // 8 * 8
        self.rest = cap - self.whole
        self.mixed = -(-2 * self.rest // 8) * 8
        self.rows = 2 * self.whole + self.mixed
        self.side = self.whole + self.mixed

    def row(self, slot, second):
        late = slot >= self.whole
        first_row = slot + jnp.where(late, 1.0 * self.whole, 0.0)
        second_row = slot + jnp.where(late, 1.0 * (self.whole + self.rest), 1.0 * self.whole)
        return jnp.where(second, second_row, first_row)


def selection(key, value, chunk):
    experts, lanes = key.shape
    slot = lax.broadcasted_iota(jnp.int32, (experts, chunk, lanes), 1)
    hit = slot == key.astype(jnp.int32)[:, None, :]
    full = jnp.where(hit, jnp.broadcast_to(value[:, None, :], hit.shape), 0.0)
    return full.reshape(experts * chunk, lanes).astype(BF16)


def pack(keys, values, both, chunk, staged, outs, sems):
    copies = []
    count = keys.shape[0]
    group = max(1, count // 2)
    for start in range(0, count, group):
        here = slice(start, start + group)
        pick = selection(keys[here], values[here], chunk)
        made = jnp.dot(pick, both, preferred_element_type=F32)
        staged[here] = made.reshape(group, chunk, -1).astype(BF16)
        for e in range(start, start + group):
            copies.append(pltpu.make_async_copy(staged.at[e], outs[e], sems.at[e]))
            copies[-1].start()
    for copy in copies:
        copy.wait()


def route_kernel(lay, sub, where, ids_in, weights_in, tok, grad, *refs):
    packed, refs = refs[:sub], refs[sub:]
    far, table, ids, weights, both, staged, turned, far_staged, in_sems, sems = refs
    rows, width = tok.shape
    loads = [
        pltpu.make_async_copy(ids_in, ids, in_sems.at[0]),
        pltpu.make_async_copy(weights_in, weights, in_sems.at[1]),
        pltpu.make_async_copy(tok, both.at[pl.ds(0, rows)], in_sems.at[2]),
        pltpu.make_async_copy(grad, both.at[pl.ds(rows, rows)], in_sems.at[3]),
    ]
    for load in loads:
        load.start()
    topk = ids.shape[0]
    experts, lanes = table.shape[1], table.shape[2]
    source = lax.broadcasted_iota(jnp.int32, (rows, lanes), 0)
    lane = lax.broadcasted_iota(jnp.int32, (rows, lanes), 1)
    target = jnp.where(lane >= rows, lane - rows, lane)
    earlier = jnp.where(source < target, 1.0, 0.0).astype(BF16)
    same = jnp.where(source == target, 1.0, 0.0).astype(BF16)
    expert = lax.broadcasted_iota(jnp.int32, (experts, rows), 0)
    named = jnp.zeros((experts, rows), F32)
    weight = jnp.zeros((experts, rows), F32)
    loads[0].wait()
    loads[1].wait()
    for k in range(topk):
        hit = ids[k : k + 1, :] == expert
        named = named + jnp.where(hit, 1.0, 0.0)
        weight = weight + jnp.where(hit, weights[k : k + 1, :].astype(F32), 0.0)
    named_b = named.astype(BF16)
    position = jnp.dot(named_b, earlier, preferred_element_type=F32)
    present = jnp.dot(named_b, same, preferred_element_type=F32)
    factor = jnp.dot(weight.astype(BF16), same, preferred_element_type=F32)
    second = lax.broadcasted_iota(jnp.int32, (experts, lanes), 1) >= rows
    table[0] = jnp.where(present > 0.5, lay.row(position, second), -1.0)
    table[1] = jnp.where(second, factor, 1.0)
    other = pl.ds(pl.multiple_of((1 - where[0]) * sub, sub), sub)
    far_staged[rows:, :lanes] = table[0, other, :].astype(BF16)
    far_staged[rows:, lanes : 2 * lanes] = table[1, other, :].astype(BF16)
    far_staged[rows:, 2 * lanes :] = jnp.zeros((sub, width - 2 * lanes), BF16)
    loads[2].wait()
    loads[3].wait()
    far_staged[:rows] = both[rows:]
    send = pltpu.make_async_copy(far_staged, far, in_sems.at[4])
    send.start()
    for offset in range(sub):
        row = pl.ds(where[0] * sub + (where[2] ^ offset), 1)
        turned[0, offset : offset + 1] = table[0, row, :]
        turned[1, offset : offset + 1] = table[1, row, :]
    pack(turned[0], turned[1], both[...], lay.rows, staged, packed, sems)
    send.wait()


def relay_kernel(lay, where, tok, far, packed, key, staged, sems):
    rows = tok.shape[0]
    lanes = key.shape[1]
    both = jnp.concatenate([tok[...], far[:rows]], axis=0)
    outs = [packed.at[e] for e in range(packed.shape[0])]
    key[...] = far[rows:, :lanes].astype(F32)
    factor = far[rows:, lanes : 2 * lanes].astype(F32)
    pack(key[...], factor, both, lay.rows, staged, outs, sems)


def split_sides(lay, got, first, second):
    for e, chunk in enumerate(got):
        at, side, whole = e * lay.side, lay.side, lay.whole
        if whole:
            first[at : at + whole] = chunk[:whole]
            second[at : at + whole] = chunk[whole : 2 * whole]
        first[at + whole : at + side] = chunk[2 * whole :]
        second[at + whole : at + side] = chunk[2 * whole :]


def align(lay, x, experts):
    parts = []
    for e in range(experts):
        at = e * lay.side
        if lay.whole:
            parts.append(x[at : at + lay.whole])
        late = x[at + lay.whole : at + lay.side]
        parts.append(pltpu.roll(late, lay.mixed - lay.rest, 0) if lay.rest else late)
    return jnp.concatenate(parts, axis=0)


def expert_kernel(lay, sub, direct, where, *refs):
    if direct:
        got, refs = refs[:sub], refs[sub:]
        w_gate, w_up, down_in, *refs = refs
        back_rows, refs = refs[:sub], refs[sub:]
    else:
        got, w_gate, w_up, down_in, back_rows, *refs = refs
        got = [got.at[e] for e in range(sub)]
        back_rows = [back_rows.at[e] for e in range(sub)]
    kept, (staged, first, second, small, down_small, w_down) = refs[:4], refs[4:10]
    kept_sems, sems, load_sem = refs[10:]
    load = pltpu.make_async_copy(down_in, w_down, load_sem)
    load.start()
    stores = [
        pltpu.make_async_copy(held, out, kept_sems.at[i])
        for i, (held, out) in enumerate(zip((first, second, small, down_small), kept))
    ]
    width, units = w_gate.shape
    total = sub * lay.side
    split_sides(lay, got, first, second)
    stores[0].start()
    stores[1].start()
    gate = jnp.dot(first[...], w_gate[...], preferred_element_type=F32)
    up = jnp.dot(first[...], w_up[...], preferred_element_type=F32)
    load.wait()
    back = jnp.dot(second[...], w_down[...], preferred_element_type=F32)
    back = align(lay, back, sub)
    slot = lax.broadcasted_iota(jnp.int32, (sub, lay.side, 128), 1).reshape(total, 128)
    filled = slot[:, :1] < lay.cap
    sig = 1.0 / (1.0 + jnp.exp(-gate))
    act = gate * sig
    hidden = jnp.where(filled, act * up, 0.0)
    grad_gate = jnp.where(filled, back * up * sig * (1.0 + gate * (1.0 - sig)), 0.0).astype(BF16)
    grad_up = jnp.where(filled, back * act, 0.0).astype(BF16)
    slot_grad = lax.dot_general(grad_gate, w_gate[...], COLS_BY_COLS, preferred_element_type=F32)
    slot_grad = slot_grad + lax.dot_general(
        grad_up, w_up[...], COLS_BY_COLS, preferred_element_type=F32
    )
    route = jnp.sum(hidden * back, axis=1, keepdims=True)
    lane = lax.broadcasted_iota(jnp.int32, (total, 128), 1)
    spread = jnp.where(lane == slot, route, 0.0).reshape(sub, lay.side, 128)
    sums = jnp.sum(spread, axis=1)
    half = width // 2
    copies = []
    early = lax.broadcasted_iota(jnp.int32, (lay.mixed, half), 0) < lay.rest
    for e in range(sub):
        at, whole = e * lay.side, lay.whole
        if whole:
            staged[e, :whole] = slot_grad[at : at + whole, :half].astype(BF16)
            staged[e, whole : 2 * whole] = slot_grad[at : at + whole, half:].astype(BF16)
        late = slot_grad[at + whole : at + lay.side]
        if lay.rest:
            mixed = jnp.where(early, late[:, :half], pltpu.roll(late[:, half:], lay.rest, 0))
            staged[e, 2 * whole : lay.rows] = mixed.astype(BF16)
        staged[e, lay.rows :, :128] = jnp.broadcast_to(sums[e : e + 1], (8, 128)).astype(BF16)
        staged[e, lay.rows :, 128:] = jnp.zeros((8, half - 128), BF16)
        copies.append(pltpu.make_async_copy(staged.at[e], back_rows[e], sems.at[e]))
        copies[-1].start()
    small[:, :units] = grad_gate
    small[:, units:] = grad_up
    stores[2].start()
    parts = []
    for e in range(sub):
        at, whole = e * lay.side, lay.whole
        if whole:
            parts.append(hidden[at : at + whole])
        late = hidden[at + whole : at + lay.side]
        parts.append(pltpu.roll(late, lay.rest, 0) if lay.rest else late)
    down_small[...] = jnp.concatenate(parts, axis=0).astype(BF16)
    stores[3].start()
    for copy in copies + stores:
        copy.wait()


def weight_kernel(replicas, where, *refs):
    sources, outs, refs = refs[:8], refs[8 : 8 + replicas], refs[8 + replicas :]
    held, (firsts, seconds, sems) = refs[:4], refs[4:]
    first, second, small, down_small = held
    width = firsts.shape[2]
    units = down_small.shape[1]
    total = sources[0].shape[0]
    loads = []
    for i in range(8):
        rows = pl.ds((i // 4) * total, total)
        loads.append(pltpu.make_async_copy(sources[i], held[i % 4].at[rows], sems.at[i]))
    for i in (0, 2, 4, 6, 1, 3, 5, 7):
        loads[i].start()
    for side, (rows_held, parts, factors, cols) in enumerate(
        ((first, firsts, small, slice(0, 2 * units)),
         (second, seconds, down_small, slice(2 * units, 3 * units)))
    ):
        for i in (side, side + 2, side + 4, side + 6):
            loads[i].wait()
        for b in range(replicas):
            parts[b] = rows_held[:, b * width : (b + 1) * width]
        for s in reversed(range(replicas)):
            b = lax.rem(where[1] + s, replicas)
            outs[s][:, cols] = lax.dot_general(
                parts[b], factors[...], ROWS_BY_ROWS, preferred_element_type=F32
            ).astype(BF16)


def update_kernel(replicas, where, *refs):
    parts, moms, outs = refs[:replicas], refs[replicas : replicas + 3], refs[replicas + 3 :]
    outs, (held, made, in_sems, out_sems) = outs[:3], outs[3:]
    units = moms[0].shape[2]
    pieces = 4 if moms[0].shape[1] % 32 == 0 else 1
    step = moms[0].shape[1] // pieces
    work = []
    for i in range(3):
        for j in range(pieces):
            rows = pl.ds(j * step, step)
            sem = 4 * i + j
            load = pltpu.make_async_copy(
                moms[i].at[0, rows], held.at[i, rows], in_sems.at[sem]
            )
            load.start()
            store = pltpu.make_async_copy(
                made.at[i, rows], outs[i].at[0, rows], out_sems.at[sem]
            )
            work.append((i, slice(j * step, (j + 1) * step), load, store))
    for i, rows, load, store in work:
        cols = slice(i * units, (i + 1) * units)
        total = parts[0][rows, cols].astype(F32)
        for part in parts[1:]:
            total = total + part[rows, cols].astype(F32)
        load.wait()
        made[i, rows] = 0.9 * held[i, rows] + 0.1 * total
        store.start()
    for *_, store in work:
        store.wait()


def gathered(key, returned):
    ones = jnp.ones(key.shape, F32)
    chunk = returned.shape[1]
    flat = returned.reshape(returned.shape[0] * chunk, returned.shape[2])
    return lax.dot_general(
        selection(key, ones, chunk), flat, ROWS_BY_ROWS, preferred_element_type=F32
    )


def route_values(lay, key, returned):
    key = jnp.where(key >= lay.whole, key - lay.whole, key).astype(jnp.int32)
    value = jnp.zeros(key.shape, F32)
    per_slot = returned[:, lay.rows, :128].astype(F32)
    for q in range(lay.cap):
        value = value + jnp.where(key == q, per_slot[:, q : q + 1], 0.0)
    return value


def partial_kernel(lay, rows, where, key, returned, out):
    sub, _, half = returned.shape
    lanes = key.shape[1]
    total = gathered(key[...], returned[...])
    out[:rows, :half] = total[:rows].astype(BF16)
    out[:rows, half:] = total[rows:].astype(BF16)
    out[rows:, :lanes] = route_values(lay, key[...], returned[...]).astype(BF16)
    out[rows:, lanes:] = jnp.zeros((sub, 2 * half - lanes), BF16)


def final_kernel(lay, sub, where, table, partial, ids, weights, *refs):
    pieces, (out, route, returned, own) = refs[:sub], refs[sub:]
    rows, half = out.shape[0], returned.shape[2]
    topk = ids.shape[0]
    for offset in range(sub):
        returned[offset] = pieces[offset][...]
        row = pl.ds(where[0] * sub + (where[2] ^ offset), 1)
        own[offset : offset + 1] = table[0, row, :]
    total = gathered(own[...], returned[...])
    out[:, :half] = (total[:rows] + partial[:rows, :half].astype(F32)).astype(BF16)
    out[:, half:] = (total[rows:] + partial[:rows, half:].astype(F32)).astype(BF16)
    near = route_values(lay, own[...], returned[...])[:, :rows]
    far = partial[rows:, :rows].astype(F32)
    expert = lax.broadcasted_iota(jnp.int32, (sub, rows), 0)
    near_expert = (expert ^ where[2]) + where[0] * sub
    far_expert = expert + (1 - where[0]) * sub
    for k in range(topk):
        name = ids[k : k + 1, :]
        picked = jnp.where(name == near_expert, near, 0.0)
        picked = picked + jnp.where(name == far_expert, far, 0.0)
        picked = jnp.sum(picked, axis=0, keepdims=True)
        route[k : k + 1, :] = (picked / weights[k : k + 1, :].astype(F32)).astype(BF16)


def per_device(
    tokens, route_ids, route_weights, out_grad, w_gate, w_up, w_down, mom_gate, mom_up, mom_down
):
    experts = lax.axis_size("expert")
    replicas = lax.axis_size("replica")
    rows, width = tokens.shape
    topk = route_ids.shape[1]
    units = w_gate.shape[2]
    lay = Layout(7 * rows * topk // (6 * experts))
    sub = experts // 2
    lanes = 2 * rows
    half = width // 2
    strip = width // replicas
    total = sub * lay.side
    me = lax.axis_index("expert")
    place = me // sub
    where = jnp.stack([place, lax.axis_index("replica"), me % sub]).astype(jnp.int32)
    groups = [list(range(sub)), list(range(sub, experts))]
    S = jax.ShapeDtypeStruct
    DMA = pltpu.SemaphoreType.DMA

    def permute(x, partner):
        return lax.ppermute(x, "expert", [(i, partner(i)) for i in range(experts)])

    def across(x):
        return permute(x, lambda i: (i + sub) % experts)

    def within(x):
        return lax.all_to_all(
            x, "expert", split_axis=0, concat_axis=0, tiled=True, axis_index_groups=groups
        )

    ids = route_ids.T
    weights = route_weights.T
    far_tok = across(tokens)
    chunk = S((lay.rows, width), BF16)
    staged = pltpu.VMEM((sub, *chunk.shape), BF16)
    *packed, far, table = call(
        functools.partial(route_kernel, lay, sub),
        [chunk] * sub + [S((rows + sub, width), BF16), S((2, experts, lanes), F32)],
        (where, ids, weights, tokens, out_grad),
        2 * sub * lay.rows * lanes * width,
        scratch=[
            pltpu.VMEM(ids.shape, ids.dtype),
            pltpu.VMEM(weights.shape, weights.dtype),
            pltpu.VMEM((2 * rows, width), BF16),
            staged,
            pltpu.VMEM((2, sub, lanes), F32),
            pltpu.VMEM((rows + sub, width), BF16),
            DMA((5,)),
            DMA((sub,)),
        ],
        streamed=(1, 2, 3, 4),
        out_streamed=range(sub + 1),
    )
    far = across(far)
    got_a = packed[:1] + [None] * (sub - 1)
    for offset in range(1, sub):
        got_a[offset] = permute(packed[offset], lambda i: i ^ offset)
    relayed, far_key = call(
        functools.partial(relay_kernel, lay),
        [S((sub, *chunk.shape), BF16), S((sub, lanes), F32)],
        (where, far_tok, far),
        2 * sub * lay.rows * lanes * width,
        scratch=[staged, DMA((sub,))],
        out_streamed=(0,),
    )
    got_b = [within(relayed)]

    def expert(got, direct):
        back = (sub, lay.rows + 8, half)
        kept = [S((total, cols), BF16) for cols in (width, width, 2 * units, units)]
        outs = ([S(back[1:], BF16)] * sub if direct else [S(back, BF16)]) + kept
        made = call(
            functools.partial(expert_kernel, lay, sub, direct),
            outs,
            (where, *got, w_gate[0], w_up[0], w_down[0]),
            10 * total * width * units,
            scratch=[pltpu.VMEM(back, BF16)]
            + [pltpu.VMEM(x.shape, BF16) for x in kept]
            + [pltpu.VMEM((width, units), BF16), DMA((4,)), DMA((sub,)), DMA],
            streamed=(len(got) + 3,),
            out_streamed=range(len(outs)),
        )
        return made[:-4], made[-4:]

    back_a, factors_a = expert(got_a, True)
    ret_a = [back_a[0]] + [None] * (sub - 1)
    for offset in range(1, sub):
        ret_a[offset] = permute(back_a[offset], lambda i: i ^ offset)
    (back_b,), factors_b = expert(got_b, False)
    ret_b = within(back_b)
    turned = pltpu.VMEM((replicas, 2 * total, strip), BF16)
    parts = call(
        functools.partial(weight_kernel, replicas),
        [S((strip, 3 * units), BF16)] * replicas,
        (where, *factors_a, *factors_b),
        12 * total * width * units,
        scratch=[pltpu.VMEM((2 * x.shape[0], x.shape[1]), BF16) for x in factors_a]
        + [turned, turned, DMA((8,))],
        streamed=range(1, 9),
        limit=16 if strip >= 128 else 48,
    )
    moved = [
        lax.ppermute(
            parts[s], "replica", [(i, (i + s) % replicas) for i in range(replicas)]
        )
        for s in range(1, replicas)
    ]
    (partial,) = call(
        functools.partial(partial_kernel, lay, rows),
        [S((rows + sub, width), BF16)],
        (where, far_key, ret_b),
        2 * sub * lay.rows * lanes * half,
    )
    partial = across(partial)
    new = call(
        functools.partial(update_kernel, replicas),
        [S(mom_gate.shape, F32)] * 3,
        (where, parts[0], *moved, mom_gate, mom_up, mom_down),
        9 * strip * units,
        scratch=[pltpu.VMEM((3, strip, units), F32)] * 2 + [DMA((12,)), DMA((12,))],
        streamed=range(replicas + 1, replicas + 4),
        out_streamed=range(3),
    )
    grad_tokens, grad_route = call(
        functools.partial(final_kernel, lay, sub),
        [S((rows, width), BF16), S((topk, rows), BF16)],
        (where, table, partial, ids, weights, *ret_a),
        2 * sub * lay.rows * lanes * half,
        scratch=[
            pltpu.VMEM((sub, lay.rows + 8, half), BF16),
            pltpu.VMEM((sub, lanes), F32),
        ],
    )
    return (grad_tokens, grad_route.T, *new)


def solution(mesh):
    tok = P(("expert", "replica"), None)
    full = P("expert", None, None)
    shard = P("expert", "replica", None)
    return jax.shard_map(
        per_device,
        mesh=mesh,
        in_specs=(tok,) * 4 + (full,) * 3 + (shard,) * 3,
        out_specs=(tok, tok, shard, shard, shard),
        check_vma=False,
    )
```

```python
import functools

import jax
import jax.numpy as jnp
from jax import lax
from jax.experimental import pallas as pl
from jax.experimental.pallas import tpu as pltpu
from jax.sharding import PartitionSpec as P


F32 = jnp.float32
BF16 = jnp.bfloat16
ROWS_BY_ROWS = (((0,), (0,)), ((), ()))
COLS_BY_COLS = (((1,), (1,)), ((), ()))
VMEM = pl.BlockSpec(memory_space=pltpu.VMEM)
SMEM = pl.BlockSpec(memory_space=pltpu.SMEM)


HBM = pl.BlockSpec(memory_space=pltpu.HBM)


def call(kernel, outs, ins, flops, scratch=(), streamed=(), out_streamed=(), limit=16):
    nbytes = sum(x.size * x.dtype.itemsize for x in list(ins[1:]) + list(outs))
    ins = [
        pltpu.with_memory_space_constraint(x, pltpu.HBM) if i in streamed else x
        for i, x in enumerate(ins)
    ]
    outs = [
        pltpu.HBM(x.shape, x.dtype) if i in out_streamed else x for i, x in enumerate(outs)
    ]
    return pl.pallas_call(
        kernel,
        out_shape=tuple(outs),
        in_specs=[SMEM] + [HBM if i in streamed else VMEM for i in range(1, len(ins))],
        out_specs=tuple(HBM if i in out_streamed else VMEM for i in range(len(outs))),
        scratch_shapes=list(scratch),
        cost_estimate=pl.CostEstimate(flops=flops, bytes_accessed=nbytes, transcendentals=0),
        compiler_params=pltpu.CompilerParams(vmem_limit_bytes=limit << 20),
    )(*ins)


class Layout:
    def __init__(self, cap):
        self.cap = cap
        self.whole = cap // 8 * 8
        self.rest = cap - self.whole
        self.mixed = -(-2 * self.rest // 8) * 8
        self.rows = 2 * self.whole + self.mixed
        self.side = self.whole + self.mixed

    def row(self, slot, second):
        late = slot >= self.whole
        first_row = slot + jnp.where(late, 1.0 * self.whole, 0.0)
        second_row = slot + jnp.where(late, 1.0 * (self.whole + self.rest), 1.0 * self.whole)
        return jnp.where(second, second_row, first_row)


def selection(key, value, chunk):
    experts, lanes = key.shape
    slot = lax.broadcasted_iota(jnp.int32, (experts, chunk, lanes), 1)
    hit = slot == key.astype(jnp.int32)[:, None, :]
    full = jnp.where(hit, jnp.broadcast_to(value[:, None, :], hit.shape), 0.0)
    return full.reshape(experts * chunk, lanes).astype(BF16)


def packed_groups(keys, values, both, chunk):
    count = keys.shape[0]
    group = max(1, count // 2)
    for start in range(0, count, group):
        here = slice(start, start + group)
        made = jnp.dot(
            selection(keys[here], values[here], chunk), both, preferred_element_type=F32
        )
        for e in range(group):
            yield start + e, made[e * chunk : (e + 1) * chunk].astype(BF16)


def route_kernel(
    lay, sub, where, ids_in, weights_in, tok, grad, packed, far, table,
    ids, weights, both, staged, far_staged, in_sems, sems,
):
    rows, width = tok.shape
    loads = [
        pltpu.make_async_copy(ids_in, ids, in_sems.at[0]),
        pltpu.make_async_copy(weights_in, weights, in_sems.at[1]),
        pltpu.make_async_copy(tok, both.at[pl.ds(0, rows)], in_sems.at[2]),
        pltpu.make_async_copy(grad, both.at[pl.ds(rows, rows)], in_sems.at[3]),
    ]
    for load in loads:
        load.start()
    topk = ids.shape[0]
    experts, lanes = table.shape[1], table.shape[2]
    source = lax.broadcasted_iota(jnp.int32, (rows, lanes), 0)
    lane = lax.broadcasted_iota(jnp.int32, (rows, lanes), 1)
    target = jnp.where(lane >= rows, lane - rows, lane)
    earlier = jnp.where(source < target, 1.0, 0.0).astype(BF16)
    same = jnp.where(source == target, 1.0, 0.0).astype(BF16)
    expert = lax.broadcasted_iota(jnp.int32, (experts, rows), 0)
    named = jnp.zeros((experts, rows), F32)
    weight = jnp.zeros((experts, rows), F32)
    loads[0].wait()
    loads[1].wait()
    for k in range(topk):
        hit = ids[k : k + 1, :] == expert
        named = named + jnp.where(hit, 1.0, 0.0)
        weight = weight + jnp.where(hit, weights[k : k + 1, :].astype(F32), 0.0)
    named_b = named.astype(BF16)
    position = jnp.dot(named_b, earlier, preferred_element_type=F32)
    present = jnp.dot(named_b, same, preferred_element_type=F32)
    factor = jnp.dot(weight.astype(BF16), same, preferred_element_type=F32)
    second = lax.broadcasted_iota(jnp.int32, (experts, lanes), 1) >= rows
    table[0] = jnp.where(present > 0.5, lay.row(position, second), -1.0)
    table[1] = jnp.where(second, factor, 1.0)
    other = pl.ds(pl.multiple_of((1 - where[0]) * sub, sub), sub)
    end = rows * (width // lanes)
    far_staged[end : end + sub] = table[0, other, :].astype(BF16)
    far_staged[end + sub :] = table[1, other, :].astype(BF16)
    loads[2].wait()
    loads[3].wait()
    for j in range(width // lanes):
        far_staged[j * rows : (j + 1) * rows] = both[rows:, j * lanes : (j + 1) * lanes]
    send = pltpu.make_async_copy(far_staged, far, in_sems.at[4])
    send.start()
    own = pl.ds(pl.multiple_of(where[0] * sub, sub), sub)
    copies = []
    for e, made in packed_groups(table[0, own, :], table[1, own, :], both[...], lay.rows):
        staged[e] = made
        copies.append(pltpu.make_async_copy(staged.at[e], packed.at[e], sems.at[e]))
        copies[-1].start()
    for copy in copies:
        copy.wait()
    send.wait()


def relay_kernel(lay, sub, where, tok, far, *refs):
    packed, (key, factor, staged, sem) = refs[:sub], refs[sub:]
    rows = tok.shape[0]
    lanes = key.shape[1]
    blocks = tok.shape[1] // lanes
    end = rows * blocks
    grad = [far[j * rows : (j + 1) * rows] for j in range(blocks)]
    both = jnp.concatenate([tok[...], jnp.concatenate(grad, axis=1)], axis=0)
    factor[0] = far[end : end + sub].astype(F32)
    factor[1] = far[end + sub :].astype(F32)
    for offset in range(sub):
        row = pl.ds(where[2] ^ offset, 1)
        key[offset : offset + 1] = factor[0, row, :]
        factor[2, offset : offset + 1] = factor[1, row, :]
    copy = pltpu.make_async_copy(staged, packed[0], sem)
    for e, made in packed_groups(key[...], factor[2], both, lay.rows):
        if e == 0:
            staged[...] = made
            copy.start()
        else:
            packed[e][...] = made
    copy.wait()


def split_sides(lay, got, first, second, arrival):
    for e in (*range(1, len(got)), 0):
        if e == 0 and arrival is not None:
            arrival.wait()
        chunk = got[e]
        at, side, whole = e * lay.side, lay.side, lay.whole
        if whole:
            first[at : at + whole] = chunk[:whole]
            second[at : at + whole] = chunk[whole : 2 * whole]
        first[at + whole : at + side] = chunk[2 * whole :]
        second[at + whole : at + side] = chunk[2 * whole :]


def align(lay, x, experts):
    parts = []
    for e in range(experts):
        at = e * lay.side
        if lay.whole:
            parts.append(x[at : at + lay.whole])
        late = x[at + lay.whole : at + lay.side]
        parts.append(pltpu.roll(late, lay.mixed - lay.rest, 0) if lay.rest else late)
    return jnp.concatenate(parts, axis=0)


def expert_kernel(lay, sub, direct, where, *refs):
    if direct:
        got, refs = refs[:sub], refs[sub:]
        w_gate, w_up, down_in, *refs = refs
        back_rows, refs = refs[:sub], refs[sub:]
    else:
        got, w_gate, w_up, down_in, back_rows, *refs = refs
        got = [got.at[e] for e in range(sub)]
        back_rows = [back_rows.at[e] for e in range(sub)]
    kept, refs = refs[:4], refs[4:]
    if direct:
        first, second, small, down_small = kept
        w_down, load_sem, local, local_sem = refs
        arrival = pltpu.make_async_copy(got[0], local, local_sem)
        arrival.start()
        got = [local] + list(got[1:])
        stores = []
    else:
        staged, first, second, small, down_small, w_down, load_sem, kept_sems, sems = refs
        stores = [
            pltpu.make_async_copy(held, out, kept_sems.at[i])
            for i, (held, out) in enumerate(zip((first, second, small, down_small), kept))
        ]
    load = pltpu.make_async_copy(down_in, w_down, load_sem)
    load.start()
    width, units = w_gate.shape
    total = sub * lay.side
    split_sides(lay, got, first, second, arrival if direct else None)
    for store in stores[:2]:
        store.start()
    gate = jnp.dot(first[...], w_gate[...], preferred_element_type=F32)
    up = jnp.dot(first[...], w_up[...], preferred_element_type=F32)
    load.wait()
    back = jnp.dot(second[...], w_down[...], preferred_element_type=F32)
    back = align(lay, back, sub)
    slot = lax.broadcasted_iota(jnp.int32, (sub, lay.side, 128), 1).reshape(total, 128)
    filled = slot[:, :1] < lay.cap
    sig = 1.0 / (1.0 + jnp.exp(-gate))
    act = gate * sig
    hidden = jnp.where(filled, act * up, 0.0)
    grad_gate = jnp.where(filled, back * up * sig * (1.0 + gate * (1.0 - sig)), 0.0).astype(BF16)
    grad_up = jnp.where(filled, back * act, 0.0).astype(BF16)
    small[:, :units] = grad_gate
    small[:, units:] = grad_up
    for store in stores[2:3]:
        store.start()
    parts = []
    for e in range(sub):
        at, whole = e * lay.side, lay.whole
        if whole:
            parts.append(hidden[at : at + whole])
        late = hidden[at + whole : at + lay.side]
        parts.append(pltpu.roll(late, lay.rest, 0) if lay.rest else late)
    down_small[...] = jnp.concatenate(parts, axis=0).astype(BF16)
    for store in stores[3:]:
        store.start()
    slot_grad = lax.dot_general(grad_gate, w_gate[...], COLS_BY_COLS, preferred_element_type=F32)
    slot_grad = slot_grad + lax.dot_general(
        grad_up, w_up[...], COLS_BY_COLS, preferred_element_type=F32
    )
    route = jnp.sum(hidden * back, axis=1, keepdims=True)
    lane = lax.broadcasted_iota(jnp.int32, (total, 128), 1)
    spread = jnp.where(lane == slot, route, 0.0).reshape(sub, lay.side, 128)
    sums = jnp.sum(spread, axis=1)
    half = width // 2
    copies = []
    staged = back_rows if direct else [staged.at[e] for e in range(sub)]
    early = lax.broadcasted_iota(jnp.int32, (lay.mixed, half), 0) < lay.rest
    for e in range(sub):
        at, whole = e * lay.side, lay.whole
        late = slot_grad[at + whole : at + lay.side]
        if lay.rest:
            late = jnp.where(early, late[:, :half], pltpu.roll(late[:, half:], lay.rest, 0))
        for j in range(half // 128):
            base, cols = j * lay.rows, slice(j * 128, (j + 1) * 128)
            others = slice(half + j * 128, half + (j + 1) * 128)
            if whole:
                staged[e][base : base + whole] = slot_grad[at : at + whole, cols].astype(BF16)
                staged[e][base + whole : base + 2 * whole] = slot_grad[
                    at : at + whole, others
                ].astype(BF16)
            if lay.rest:
                staged[e][base + 2 * whole : base + lay.rows] = late[:, cols].astype(BF16)
        end = lay.rows * (half // 128)
        staged[e][end:] = jnp.broadcast_to(sums[e : e + 1], (8, 128)).astype(BF16)
        if not direct:
            copies.append(pltpu.make_async_copy(staged[e], back_rows[e], sems.at[e]))
            copies[-1].start()
    for copy in copies + stores:
        copy.wait()


def weight_parts(where, held, turned, replicas):
    first, second, small, down_small = held
    width = turned.shape[3]
    for b in range(replicas):
        turned[0, b] = first[:, b * width : (b + 1) * width]
        turned[1, b] = second[:, b * width : (b + 1) * width]
    for s in reversed(range(replicas)):
        b = lax.rem(where[1] + s, replicas)
        for side, factors in enumerate((small, down_small)):
            at = side * small.shape[1]
            yield s, slice(at, at + factors.shape[1]), lax.dot_general(
                turned[side, b], factors[...], ROWS_BY_ROWS, preferred_element_type=F32
            )


def weight_kernel(replicas, where, *refs):
    sources, here, outs, refs = refs[:4], refs[4:8], refs[8 : 8 + replicas], refs[8 + replicas :]
    held, (turned, sums, sems) = refs[:4], refs[4:]
    loads = [pltpu.make_async_copy(sources[i], held[i], sems.at[i]) for i in range(4)]
    for load in loads:
        load.start()
    for s, cols, made in weight_parts(where, here, turned, replicas):
        sums[s, :, cols] = made
    for load in loads:
        load.wait()
    for s, cols, made in weight_parts(where, held, turned, replicas):
        outs[s][:, cols] = (sums[s, :, cols] + made).astype(BF16)


def pieces_of(rows):
    count = 4 if rows % 32 == 0 else 1
    step = rows // count
    return [slice(j * step, (j + 1) * step) for j in range(count)]


def decay_kernel(where, part, *refs):
    moms, (made, sems) = refs[:3], refs[3:]
    units = made.shape[2]
    pieces = pieces_of(made.shape[1])
    work = []
    for i in range(3):
        for j, rows in enumerate(pieces):
            load = pltpu.make_async_copy(
                moms[i].at[0, rows], made.at[i, rows], sems.at[4 * i + j]
            )
            load.start()
            work.append((i, rows, load))
    for i, rows, load in work:
        own = 0.1 * part[rows, i * units : (i + 1) * units].astype(F32)
        load.wait()
        made[i, rows] = 0.9 * made[i, rows] + own


def update_kernel(where, decayed, *refs):
    parts, (*outs, made, sems) = refs[:-5], refs[-5:]
    units = made.shape[2]
    stores = []
    for i in range(3):
        cols = slice(i * units, (i + 1) * units)
        for j, rows in enumerate(pieces_of(made.shape[1])):
            total = parts[0][rows, cols].astype(F32)
            for part in parts[1:]:
                total = total + part[rows, cols].astype(F32)
            made[i, rows] = decayed[i, rows] + 0.1 * total
            stores.append(
                pltpu.make_async_copy(
                    made.at[i, rows], outs[i].at[0, rows], sems.at[4 * i + j]
                )
            )
            stores[-1].start()
    for store in stores:
        store.wait()


def gathered(key, returned):
    ones = jnp.ones(key.shape, F32)
    chunk = returned.shape[1]
    flat = returned.reshape(returned.shape[0] * chunk, returned.shape[2])
    return lax.dot_general(
        selection(key, ones, chunk), flat, ROWS_BY_ROWS, preferred_element_type=F32
    )


def assemble(lay, pieces, returned, slots):
    end = lay.rows * (returned.shape[2] // 128)
    for e, piece in enumerate(pieces):
        for j in range(returned.shape[2] // 128):
            block = piece[j * lay.rows : (j + 1) * lay.rows]
            returned[e, :, j * 128 : (j + 1) * 128] = block
        slots[e : e + 1] = piece[end:].astype(F32)[:1]


def route_values(lay, key, slots):
    key = jnp.where(key >= lay.whole, key - lay.whole, key).astype(jnp.int32)
    value = jnp.zeros(key.shape, F32)
    for q in range(lay.cap):
        value = value + jnp.where(key == q, slots[:, q : q + 1], 0.0)
    return value


def partial_kernel(lay, sub, where, key, *refs):
    pieces, (out, returned, slots) = refs[:sub], refs[sub:]
    lanes = key.shape[1]
    rows = lanes // 2
    assemble(lay, pieces, returned, slots)
    total = gathered(key[...], returned[...]).astype(BF16)
    blocks = returned.shape[2] // lanes
    for j in range(blocks):
        cols = slice(j * lanes, (j + 1) * lanes)
        out[j * rows : (j + 1) * rows] = total[:rows, cols]
        out[(blocks + j) * rows : (blocks + j + 1) * rows] = total[rows:, cols]
    out[2 * blocks * rows :] = route_values(lay, key[...], slots[...]).astype(BF16)


def final_kernel(
    lay, sub, where, table, partial, ids, weights, arrived, out, route, returned, slots
):
    rows, half = out.shape[0], returned.shape[2]
    lanes = partial.shape[1]
    topk = ids.shape[0]
    own = table[0, pl.ds(pl.multiple_of(where[0] * sub, sub), sub), :]
    assemble(lay, [arrived.at[e] for e in range(sub)], returned, slots)
    total = gathered(own, returned[...])
    blocks = half // lanes
    for j in range(2 * blocks):
        side = total[rows:] if j >= blocks else total[:rows]
        cols = slice((j % blocks) * lanes, (j % blocks + 1) * lanes)
        far = partial[j * rows : (j + 1) * rows].astype(F32)
        out[:, j * lanes : (j + 1) * lanes] = (side[:, cols] + far).astype(BF16)
    near = route_values(lay, own, slots[...])[:, :rows]
    far = partial[2 * blocks * rows :].astype(F32)[:, :rows]
    expert = lax.broadcasted_iota(jnp.int32, (sub, rows), 0)
    near_expert = expert + where[0] * sub
    far_expert = (expert ^ where[2]) + (1 - where[0]) * sub
    for k in range(topk):
        name = ids[k : k + 1, :]
        picked = jnp.where(name == near_expert, near, 0.0)
        picked = picked + jnp.where(name == far_expert, far, 0.0)
        picked = jnp.sum(picked, axis=0, keepdims=True)
        route[k : k + 1, :] = (picked / weights[k : k + 1, :].astype(F32)).astype(BF16)


def per_device(
    tokens, route_ids, route_weights, out_grad, w_gate, w_up, w_down, mom_gate, mom_up, mom_down
):
    experts = lax.axis_size("expert")
    replicas = lax.axis_size("replica")
    rows, width = tokens.shape
    topk = route_ids.shape[1]
    units = w_gate.shape[2]
    lay = Layout(7 * rows * topk // (6 * experts))
    sub = experts // 2
    lanes = 2 * rows
    half = width // 2
    strip = width // replicas
    total = sub * lay.side
    me = lax.axis_index("expert")
    place = me // sub
    where = jnp.stack([place, lax.axis_index("replica"), me % sub]).astype(jnp.int32)
    groups = [list(range(sub)), list(range(sub, experts))]
    S = jax.ShapeDtypeStruct
    DMA = pltpu.SemaphoreType.DMA

    def permute(x, partner):
        return lax.ppermute(x, "expert", [(i, partner(i)) for i in range(experts)])

    def across(x):
        return permute(x, lambda i: (i + sub) % experts)

    def within(x):
        return lax.all_to_all(
            x, "expert", split_axis=0, concat_axis=0, tiled=True, axis_index_groups=groups
        )

    ids = route_ids.T
    weights = route_weights.T
    far_tok = across(tokens)
    chunk = S((lay.rows, width), BF16)
    blocks = width // lanes
    far_rows = S((rows * blocks + 2 * sub, lanes), BF16)
    staged = pltpu.VMEM((sub, *chunk.shape), BF16)
    packed, far, table = call(
        functools.partial(route_kernel, lay, sub),
        [S((sub, *chunk.shape), BF16), far_rows, S((2, experts, lanes), F32)],
        (where, ids, weights, tokens, out_grad),
        2 * sub * lay.rows * lanes * width,
        scratch=[
            pltpu.VMEM(ids.shape, ids.dtype),
            pltpu.VMEM(weights.shape, weights.dtype),
            pltpu.VMEM((2 * rows, width), BF16),
            staged,
            pltpu.VMEM(far_rows.shape, BF16),
            DMA((5,)),
            DMA((sub,)),
        ],
        streamed=(1, 2, 3, 4),
        out_streamed=(0, 1),
    )
    far = across(far)
    got_a = [within(packed)]
    *relayed, far_key = call(
        functools.partial(relay_kernel, lay, sub),
        [chunk] * sub + [S((sub, lanes), F32)],
        (where, far_tok, far),
        2 * sub * lay.rows * lanes * width,
        scratch=[pltpu.VMEM((3, sub, lanes), F32), pltpu.VMEM(chunk.shape, BF16), DMA],
        out_streamed=(0,),
    )

    def swap_all(pieces):
        swapped = [pieces[0]]
        for offset in range(1, sub):
            swapped.append(permute(pieces[offset], lambda i: i ^ offset))
        return swapped

    got_b = swap_all(relayed)

    def expert(got, direct):
        back = (sub, lay.rows * (half // 128) + 8, 128)
        kept = [S((total, cols), BF16) for cols in (width, width, 2 * units, units)]
        outs = ([S(back[1:], BF16)] * sub if direct else [S(back, BF16)]) + kept
        made = call(
            functools.partial(expert_kernel, lay, sub, direct),
            outs,
            (where, *got, w_gate[0], w_up[0], w_down[0]),
            10 * total * width * units,
            scratch=([] if direct else [pltpu.VMEM(x.shape, BF16) for x in outs])
            + [pltpu.VMEM((width, units), BF16), DMA]
            + ([pltpu.VMEM(chunk.shape, BF16), DMA] if direct else [DMA((4,)), DMA((sub,))]),
            streamed=(1, len(got) + 3) if direct else (len(got) + 3,),
            out_streamed=() if direct else range(5),
        )
        return made[:-4], made[-4:]

    (back_a,), factors_a = expert(got_a, False)
    ret_a = within(back_a)
    limit = 20 if strip >= 128 else 40
    turned = pltpu.VMEM((2, replicas, total, strip), BF16)
    back_b, factors_b = expert(got_b, True)
    ret_b = swap_all(back_b)
    parts = call(
        functools.partial(weight_kernel, replicas),
        [S((strip, 3 * units), BF16)] * replicas,
        (where, *factors_a, *factors_b),
        12 * total * width * units,
        scratch=[pltpu.VMEM(x.shape, BF16) for x in factors_a]
        + [turned, pltpu.VMEM((replicas, strip, 3 * units), F32), DMA((4,))],
        streamed=range(1, 5),
        limit=limit,
    )
    moved = [
        lax.ppermute(
            parts[s], "replica", [(i, (i + s) % replicas) for i in range(replicas)]
        )
        for s in range(1, replicas)
    ]
    (partial,) = call(
        functools.partial(partial_kernel, lay, sub),
        [S((rows * blocks + sub, lanes), BF16)],
        (where, far_key, *ret_b),
        2 * sub * lay.rows * lanes * half,
        scratch=[pltpu.VMEM((sub, lay.rows, half), BF16), pltpu.VMEM((sub, 128), F32)],
    )
    partial = across(partial)
    state = pltpu.VMEM((3, strip, units), F32)
    (decayed,) = call(
        decay_kernel,
        [S((3, strip, units), F32)],
        (where, parts[0], mom_gate, mom_up, mom_down),
        6 * strip * units,
        scratch=[DMA((12,))],
        streamed=(2, 3, 4),
    )
    new = call(
        update_kernel,
        [S(mom_gate.shape, F32)] * 3,
        (where, decayed, *moved),
        6 * strip * units,
        scratch=[state, DMA((12,))],
        out_streamed=range(3),
    )
    grad_tokens, grad_route = call(
        functools.partial(final_kernel, lay, sub),
        [S((rows, width), BF16), S((topk, rows), BF16)],
        (where, table, partial, ids, weights, ret_a),
        2 * sub * lay.rows * lanes * half,
        scratch=[pltpu.VMEM((sub, lay.rows, half), BF16), pltpu.VMEM((sub, 128), F32)],
    )
    return (grad_tokens, grad_route.T, *new)


def solution(mesh):
    tok = P(("expert", "replica"), None)
    full = P("expert", None, None)
    shard = P("expert", "replica", None)
    return jax.shard_map(
        per_device,
        mesh=mesh,
        in_specs=(tok,) * 4 + (full,) * 3 + (shard,) * 3,
        out_specs=(tok, tok, shard, shard, shard),
        check_vma=False,
    )
```
